32 devices in a mesh: wide: 8 (over z, x), narrow: 4 (over y, core).
Axes of the slice: x: 2, y: 2, z: 4, core: 2. Of those that a mesh axis runs over, the one named last changes fastest.
Arguments:
- sources: float32 [64, 128, 512], P('wide', 'narrow'), may hold values from -5 to 5
- permeability: float32 [64, 128, 512], P('wide', 'narrow'), may hold values from 0.1 to 10
Outputs:
- pressure: float32 [64, 128, 512], P('wide', 'narrow')
The draws below stay inside these ranges and needn't reach their ends.
All inputs are finite; a program needn't handle non-finite values.
Results may differ from the reference program's by a relative error of at most 0.0001.
Values sent between devices are 32-bit elements; how exact they have to be, the bound alone decides.
A program may use at most 128 MiB of HBM per device.

```python
import math
import jax
import jax.numpy as jnp
from jax import lax

NZ = 512
LEVELS = 3
CSWEEPS = 16
NX = 64
NY = 128


def draw_sources(key, part):
    return jnp.clip(jax.random.normal(key, (NX, NY, NZ), jnp.float32), -5.0, 5.0)


def block_levels(key, shape, pieces, least, largest):
    loudness, own = 1.0, jax.random.fold_in(key, 6)
    for dim, parts in pieces:
        heights = jnp.exp(jax.random.uniform(jax.random.fold_in(own, dim), (parts,), jnp.float32, least / len(pieces), largest / len(pieces)))
        loudness = loudness * jnp.repeat(heights, shape[dim] // parts).reshape([-1 if axis == dim else 1 for axis in range(len(shape))])
    return loudness


def setup_inputs(seed: int = 0) -> dict:
    arg_keys = jax.random.split(jax.random.key(seed), 3)
    sources = draw_sources(jax.random.fold_in(arg_keys[2], 71), 0)
    permeability = jnp.clip(jnp.exp(math.log(10.0) - 4.6051702 * jax.random.uniform(arg_keys[1], (NX, NY, NZ), jnp.float32) ** block_levels(arg_keys[1], (NX, NY, NZ), ((0, 8), (1, 4)), -0.2, 0.2)), 0.1, 10.0)
    return {"sources": sources, "permeability": permeability}


def pad_zeros(array):
    return jnp.pad(array, 1)


def restrict(array):
    first, second, third = array.shape
    blocks = array.reshape(first // 2, 2, second // 2, 2, third // 2, 2)
    return jnp.sum(blocks, axis=(1, 3, 5)) * 0.125


def prolong(array):
    return jnp.repeat(jnp.repeat(jnp.repeat(array, 2, 0), 2, 1), 2, 2)


def centre(padded):
    return padded[1:-1, 1:-1, 1:-1]


def shifted_faces(padded):
    return [padded[2:, 1:-1, 1:-1], padded[:-2, 1:-1, 1:-1], padded[1:-1, 2:, 1:-1],
            padded[1:-1, :-2, 1:-1], padded[1:-1, 1:-1, 2:], padded[1:-1, 1:-1, :-2]]


def diagonal_of(perm_padded):
    middle = centre(perm_padded)
    result = None
    for shifted in shifted_faces(perm_padded):
        term = 0.5 * (middle + shifted)
        result = term if result is None else result + term
    return result


def neighbour_sum(perm_padded, field_padded):
    middle = centre(perm_padded)
    result = None
    for shifted, values in zip(shifted_faces(perm_padded), shifted_faces(field_padded)):
        term = 0.5 * (middle + shifted) * values
        result = term if result is None else result + term
    return result


def parity_mask(shape):
    first_index = lax.broadcasted_iota(jnp.int32, shape, 0)
    second_index = lax.broadcasted_iota(jnp.int32, shape, 1)
    third_index = lax.broadcasted_iota(jnp.int32, shape, 2)
    return (first_index + second_index + third_index) % 2 == 0


def relax_cells(pressure, perm_padded, diagonal, scaled, cells):
    updated = (scaled + neighbour_sum(perm_padded, pad_zeros(pressure))) / diagonal
    return jnp.where(cells, updated, pressure)


def reference(sources, permeability):
    right_side = sources
    perm_now = permeability
    stored = []
    for coarsening in range(LEVELS):
        square_spacing = float(4 ** coarsening)
        perm_padded = pad_zeros(perm_now)
        diagonal = diagonal_of(perm_padded)
        red_cells = parity_mask(right_side.shape)
        black_cells = jnp.logical_not(red_cells)
        scaled = square_spacing * right_side
        pressure = jnp.where(red_cells, scaled / diagonal, jnp.float32(0.0))
        pressure = relax_cells(pressure, perm_padded, diagonal, scaled, black_cells)
        residual = right_side - (pressure * diagonal - neighbour_sum(perm_padded, pad_zeros(pressure))) / square_spacing
        stored.append((pressure, perm_padded, diagonal, right_side))
        right_side = restrict(residual)
        perm_now = restrict(perm_now)
    square_spacing = float(4 ** LEVELS)
    perm_padded = pad_zeros(perm_now)
    diagonal = diagonal_of(perm_padded)
    red_cells = parity_mask(right_side.shape)
    black_cells = jnp.logical_not(red_cells)
    scaled = square_spacing * right_side
    pressure = jnp.where(red_cells, scaled / diagonal, jnp.float32(0.0))
    pressure = relax_cells(pressure, perm_padded, diagonal, scaled, black_cells)

    def sweep_pair(sweep_count, current):
        current = relax_cells(current, perm_padded, diagonal, scaled, red_cells)
        return relax_cells(current, perm_padded, diagonal, scaled, black_cells)

    correction = lax.fori_loop(0, CSWEEPS - 1, sweep_pair, pressure)
    for coarsening in reversed(range(LEVELS)):
        pressure, perm_padded, diagonal, right_side = stored[coarsening]
        square_spacing = float(4 ** coarsening)
        scaled = square_spacing * right_side
        red_cells = parity_mask(right_side.shape)
        black_cells = jnp.logical_not(red_cells)
        pressure = pressure + prolong(correction)
        pressure = relax_cells(pressure, perm_padded, diagonal, scaled, red_cells)
        correction = relax_cells(pressure, perm_padded, diagonal, scaled, black_cells)
    return correction
```

```python
import functools

import jax
import jax.numpy as jnp
from jax import lax
from jax.experimental import pallas as pl
from jax.experimental.pallas import tpu as pltpu
from jax.sharding import PartitionSpec as P

CSWEEPS = 16
F32 = jnp.float32
MESH = pl.DeviceIdType.MESH
K0, V0A, V0B, V0C, K1, V1A, V1B, V1C, V1D = range(9)


def iota(shape, dim):
    return lax.broadcasted_iota(jnp.int32, shape, dim)


def red_cells(shape, plane):
    total = iota(shape, 0) + iota(shape, 1) + plane
    return (total & 1) == 0


def matmul(left, right):
    return jnp.dot(left, right, precision=lax.Precision.HIGHEST, preferred_element_type=F32)


def each_plane(count, step, body):
    if count == step:
        for i in range(count):
            body(i)
        return

    @pl.loop(0, count // step)
    def _(chunk):
        for i in range(step):
            body(chunk * step + i)


def shift(array, amount, axis):
    return pltpu.roll(array, amount % array.shape[axis], axis)


def coefficients(kpad, weights, diag, scaled, right, square, rows, count, step):
    def body(i):
        k = kpad[i + 1, 8 : 8 + rows, :]
        lane = iota(k.shape, 1)
        last = k.shape[1] - 1
        up = jnp.where(lane == last, 0.0, shift(k, -1, 1))
        down = jnp.where(lane == 0, 0.0, shift(k, 1, 1))
        faces = [
            kpad[i + 2, 8 : 8 + rows, :],
            kpad[i, 8 : 8 + rows, :],
            kpad[i + 1, 9 : 9 + rows, :],
            kpad[i + 1, 7 : 7 + rows, :],
            up,
            down,
        ]
        faces = [0.5 * (k + face) for face in faces]
        total = functools.reduce(lambda a, b: a + b, faces)
        inverse = 1.0 / total
        for n, face in enumerate(faces):
            w = face * inverse
            if n == 4:
                w = jnp.where(lane == last, 0.0, w)
            if n == 5:
                w = jnp.where(lane == 0, 0.0, w)
            weights[n, i] = w
        diag[i] = total * (1.0 / square)
        if right is not None:
            scaled[i] = (square * inverse) * right[i]
        else:
            scaled[i] = square * inverse

    each_plane(count, step, body)


def updated(vpad, weights, scaled, i, rows):
    v = vpad[i + 1, 8 : 8 + rows, :]
    a = weights[0, i] * vpad[i + 2, 8 : 8 + rows, :] + weights[1, i] * vpad[i, 8 : 8 + rows, :]
    b = (
        weights[2, i] * vpad[i + 1, 9 : 9 + rows, :]
        + weights[3, i] * vpad[i + 1, 7 : 7 + rows, :]
    )
    c = weights[4, i] * shift(v, -1, 1) + weights[5, i] * shift(v, 1, 1)
    return v, (scaled[i] + a) + (b + c)


def first_red(vpad, scaled, rows, count, step):
    def body(i):
        s = scaled[i]
        vpad[i + 1, 8 : 8 + rows, :] = jnp.where(red_cells(s.shape, i), s, 0.0)

    each_plane(count, step, body)


def half_sweep(vpad, weights, scaled, rows, count, step, red, out=None):
    def body(i):
        v, new = updated(vpad, weights, scaled, i, rows)
        cells = red_cells(v.shape, i)
        value = jnp.where(cells, new, v) if red else jnp.where(cells, v, new)
        if out is None:
            vpad[i + 1, 8 : 8 + rows, :] = value
        else:
            out[i] = value

    each_plane(count, step, body)


def restrict_pair(first, second, tmp, slot):
    half = first.shape[0] // 2
    total = first + second
    parts = []
    for c in range(first.shape[1] // 128):
        tmp[slot, c, : 2 * half, :] = total[:, c * 128 : (c + 1) * 128]
        parts.append(tmp[slot, c, pl.ds(0, half, 2), :] + tmp[slot, c, pl.ds(1, half, 2), :])
    return parts


def kernel(sizes, b_ref, k_ref, out_ref, *s):
    wn, nn = sizes
    (kp0, v0, w0, d0, s0, kp1, v1, w1, d1, s1, b1, k1, kp2, v2, w2, d2, s2, f2, b2l, k2l,
     gk, gb, w3, s3, tmp, half0, half1, half2, up0, up1, up2, rmat, pmat,
     ws0, wr0, ns0, nr0, ws1, wr1, ns1, nr1,
     hs, hr, gsa, gra, gsb, grb) = s
    x0, y0, z0 = b_ref.shape
    x1, y1, z1 = x0 // 2, y0 // 2, z0 // 2
    x2, y2, z2 = x1 // 2, y1 // 2, z1 // 2
    gx, gy = x2 * wn, y2 * nn
    px = gx // 4
    y3 = gy // 2
    w, n = lax.axis_index("wide"), lax.axis_index("narrow")

    def wide(d):
        return (lax.rem(w + d, wn), n)

    def narrow(d):
        return (w, lax.rem(n + d, nn))

    barrier = pltpu.get_barrier_semaphore()
    for d in range(1, wn):
        pl.semaphore_signal(barrier, inc=1, device_id=wide(d), device_id_type=MESH)
    for d in range(1, nn):
        pl.semaphore_signal(barrier, inc=1, device_id=narrow(d), device_id_type=MESH)

    rmat[...] = jnp.where(iota((256, 128), 0) // 2 == iota((256, 128), 1), 1.0, 0.0)
    pmat[...] = jnp.where(iota((128, 256), 0) == iota((128, 256), 1) // 2, 1.0, 0.0)
    for pad, rows in ((kp0, y0), (v0, y0), (kp1, y1), (v1, y1), (kp2, gy), (v2, gy)):
        planes = pad.shape[0]
        zero = jnp.zeros(pad.shape[1:], F32)
        strip = jnp.zeros((8, pad.shape[2]), F32)
        pad[0] = zero
        pad[planes - 1] = zero

        @pl.loop(1, planes - 1)
        def _(i, pad=pad, rows=rows, strip=strip):
            pad[i, 0:8, :] = strip
            pad[i, 8 + rows : 16 + rows, :] = strip

    for i in range(x0):
        ns0[K0, 0, i : i + 1, :] = k_ref[i, 0:1, :]
        ns0[K0, 1, i : i + 1, :] = k_ref[i, y0 - 1 : y0, :]

    pl.semaphore_wait(barrier, wn - 1 + nn - 1)

    def halo(rnd, level, direct=None):
        base = 0 if level == 0 else K1
        ws, wr, ns, nr = (ws0, wr0, ns0, nr0) if level == 0 else (ws1, wr1, ns1, nr1)
        r = rnd - base
        specs = []
        for side in (0, 1):
            src = ws.at[r, side] if direct is None else direct.at[(0, x0 - 1)[side]]
            specs.append((
                w > 0 if side == 0 else w < wn - 1,
                w < wn - 1 if side == 0 else w > 0,
                pltpu.make_async_remote_copy(
                    src_ref=src, dst_ref=wr.at[r, 1 - side],
                    send_sem=hs.at[rnd, side], recv_sem=hr.at[rnd, side],
                    device_id=wide(wn - 1 if side == 0 else 1), device_id_type=MESH),
            ))
            specs.append((
                n > 0 if side == 0 else n < nn - 1,
                n < nn - 1 if side == 0 else n > 0,
                pltpu.make_async_remote_copy(
                    src_ref=ns.at[r, side], dst_ref=nr.at[r, 1 - side],
                    send_sem=hs.at[rnd, 2 + side], recv_sem=hr.at[rnd, 2 + side],
                    device_id=narrow(nn - 1 if side == 0 else 1), device_id_type=MESH),
            ))
        return specs

    def halo_start(rnd, level, pad=None, direct=None):
        if pad is not None:
            ws, ns = (ws0, ns0) if level == 0 else (ws1, ns1)
            r = rnd - (0 if level == 0 else K1)
            count, rows = (x0, y0) if level == 0 else (x1, y1)
            ws[r, 0] = pad[1, 8 : 8 + rows, :]
            ws[r, 1] = pad[count, 8 : 8 + rows, :]
            for i in range(count):
                ns[r, 0, i : i + 1, :] = pad[i + 1, 8:9, :]
                ns[r, 1, i : i + 1, :] = pad[i + 1, 7 + rows : 8 + rows, :]
        for sends, _, copy in halo(rnd, level, direct):
            @pl.when(sends)
            def _(copy=copy):
                copy.start()

    def halo_finish(rnd, level, pad, direct=None):
        wr, nr = (wr0, nr0) if level == 0 else (wr1, nr1)
        r = rnd - (0 if level == 0 else K1)
        count, rows = (x0, y0) if level == 0 else (x1, y1)
        for sends, receives, copy in halo(rnd, level, direct):
            @pl.when(sends)
            def _(copy=copy):
                copy.wait_send()

            @pl.when(receives)
            def _(copy=copy):
                copy.wait_recv()

        @pl.when(w > 0)
        def _():
            pad[0, 8 : 8 + rows, :] = wr[r, 0]

        @pl.when(w < wn - 1)
        def _():
            pad[count + 1, 8 : 8 + rows, :] = wr[r, 1]

        @pl.when(n > 0)
        def _():
            for i in range(count):
                pad[i + 1, 7:8, :] = nr[r, 0, i : i + 1, :]

        @pl.when(n < nn - 1)
        def _():
            for i in range(count):
                pad[i + 1, 8 + rows : 9 + rows, :] = nr[r, 1, i : i + 1, :]

    def gather_wide(g, which, local):
        copies = []
        for d in range(1, wn):
            copies.append(pltpu.make_async_remote_copy(
                src_ref=local, dst_ref=g.at[w, n],
                send_sem=gsa.at[which, d - 1], recv_sem=gra.at[which, d - 1],
                device_id=wide(d), device_id_type=MESH))
        return copies

    def gather_narrow(g, which):
        copies = []
        for d in range(1, nn):
            copies.append(pltpu.make_async_remote_copy(
                src_ref=g.at[:, n], dst_ref=g.at[:, n],
                send_sem=gsb.at[which, d - 1], recv_sem=grb.at[which, d - 1],
                device_id=narrow(d), device_id_type=MESH))
        return copies

    halo_start(K0, 0, direct=k_ref)

    for i in range(x1):
        for c, part in enumerate(restrict_pair(k_ref[2 * i], k_ref[2 * i + 1], tmp, i % 2)):
            half0[i, :, pl.ds(c * 128, 128)] = part

    def lanes_down(half, store, planes, rows, cols):
        flat = half[...].reshape(planes * rows, cols)
        for c in range(cols // 256):
            got = matmul(flat[:, c * 256 : (c + 1) * 256], rmat[...]) * 0.125
            store(c, got.reshape(planes, rows, 128))

    def store_k1(c, got):
        k1[:, :, pl.ds(c * 128, 128)] = got
        kp1[1 : 1 + x1, 8 : 8 + y1, pl.ds(c * 128, 128)] = got

    lanes_down(half0, store_k1, x1, y1, z0)
    halo_start(K1, 1, pad=kp1)
    for i in range(x2):
        for c, part in enumerate(restrict_pair(k1[2 * i], k1[2 * i + 1], tmp, i % 2)):
            half1[i, :, pl.ds(c * 128, 128)] = part

    def store_k2(c, got):
        k2l[...] = got
        gk[w, n] = got

    lanes_down(half1, store_k2, x2, y2, z1)
    k_wide = gather_wide(gk, 0, k2l)
    for copy in k_wide:
        copy.start()

    @pl.loop(0, x0)
    def _(i):
        kp0[i + 1, 8 : 8 + y0, :] = k_ref[i]

    halo_finish(K0, 0, kp0, direct=k_ref)
    coefficients(kp0, w0, d0, s0, b_ref, 1.0, y0, x0, 1)
    first_red(v0, s0, y0, x0, 1)
    halo_start(V0A, 0, pad=v0)
    halo_finish(K1, 1, kp1)
    coefficients(kp1, w1, d1, s1, None, 4.0, y1, x1, x1)
    halo_finish(V0A, 0, v0)
    half_sweep(v0, w0, s0, y0, x0, 1, False)
    halo_start(V0B, 0, pad=v0)
    for copy in k_wide:
        copy.wait()
    k_narrow = gather_narrow(gk, 0)
    for copy in k_narrow:
        copy.start()
    halo_finish(V0B, 0, v0)

    def residual(vpad, weights, scaled, diag, i, rows):
        v, new = updated(vpad, weights, scaled, i, rows)
        return diag[i] * (new - v)

    @pl.loop(0, x1)
    def _(i):
        first = residual(v0, w0, s0, d0, 2 * i, y0)
        second = residual(v0, w0, s0, d0, 2 * i + 1, y0)
        for c, part in enumerate(restrict_pair(first, second, tmp, 0)):
            half0[i, :, pl.ds(c * 128, 128)] = part

    def store_b1(c, got):
        b1[:, :, pl.ds(c * 128, 128)] = got

    lanes_down(half0, store_b1, x1, y1, z0)

    for i in range(x1):
        s1[i] = s1[i] * b1[i]
    first_red(v1, s1, y1, x1, x1)
    halo_start(V1A, 1, pad=v1)
    halo_finish(V1A, 1, v1)
    half_sweep(v1, w1, s1, y1, x1, x1, False)
    halo_start(V1B, 1, pad=v1)
    for copy in k_narrow:
        copy.wait()
    for a in range(wn):
        for c in range(nn):
            kp2[1 + a * x2 : 1 + (a + 1) * x2, 8 + c * y2 : 8 + (c + 1) * y2, :] = gk[a, c]
    halo_finish(V1B, 1, v1)
    for i in range(x2):
        first = residual(v1, w1, s1, d1, 2 * i, y1)
        second = residual(v1, w1, s1, d1, 2 * i + 1, y1)
        for c, part in enumerate(restrict_pair(first, second, tmp, i % 2)):
            half1[i, :, pl.ds(c * 128, 128)] = part

    def store_b2(c, got):
        b2l[...] = got
        gb[w, n] = got

    lanes_down(half1, store_b2, x2, y2, z1)
    b_wide = gather_wide(gb, 1, b2l)
    for copy in b_wide:
        copy.start()

    coefficients(kp2, w2, d2, f2, None, 16.0, gy, gx, 4)

    def pack_down(get, tag):
        @pl.loop(0, px)
        def _(i):
            for h in (0, 1):
                part = restrict_pair(*get(i + h * px), tmp, h)[0]
                half2[i, :, pl.ds(h * 128, 128)] = part

        return matmul(half2[...].reshape(px * y3, 256), rmat[...]).reshape(px, y3, 128) * 0.125

    def plane_of(i):
        return kp2[1 + 2 * i, 8 : 8 + gy, :], kp2[2 + 2 * i, 8 : 8 + gy, :]

    k3 = pack_down(plane_of, 0)
    shape3 = (px, y3, 128)
    p_at, r_at, l_at = iota(shape3, 0), iota(shape3, 1), iota(shape3, 2)
    z_at = l_at & 63
    outside = [
        (p_at == px - 1) & (l_at >= 64),
        (p_at == 0) & (l_at < 64),
        r_at == y3 - 1,
        r_at == 0,
        z_at == 63,
        z_at == 0,
    ]

    def neighbours(v):
        xp = jnp.concatenate([v[1:], shift(v[:1], 64, 2)], axis=0)
        xm = jnp.concatenate([shift(v[-1:], 64, 2), v[:-1]], axis=0)
        return [xp, xm, shift(v, -1, 1), shift(v, 1, 1), shift(v, -1, 2), shift(v, 1, 2)]

    faces3 = [
        0.5 * (k3 + jnp.where(out, 0.0, near)) for out, near in zip(outside, neighbours(k3))
    ]
    total3 = functools.reduce(lambda a, b: a + b, faces3)
    inverse3 = 1.0 / total3
    for m in range(6):
        w3[m] = jnp.where(outside[m], 0.0, faces3[m] * inverse3)
    s3[...] = 64.0 * inverse3

    for copy in b_wide:
        copy.wait()
    b_narrow = gather_narrow(gb, 1)
    for copy in b_narrow:
        copy.start()
    for copy in b_narrow:
        copy.wait()

    for a in range(wn):
        for c in range(nn):
            for i in range(x2):
                rows = pl.ds(c * y2, y2)
                s2[a * x2 + i, rows, :] = f2[a * x2 + i, rows, :] * gb[a, c, i]
    first_red(v2, s2, gy, gx, 4)
    half_sweep(v2, w2, s2, gy, gx, 4, False)

    def resid2(i):
        return (residual(v2, w2, s2, d2, 2 * i, gy), residual(v2, w2, s2, d2, 2 * i + 1, gy))

    b3 = pack_down(resid2, 1)
    scaled3 = s3[...] * b3
    s3[...] = scaled3
    first_at = p_at + jnp.where(l_at >= 64, px, 0)
    red3 = ((first_at + r_at + z_at) & 1) == 0

    def sweep3(e, red):
        near = neighbours(e)
        terms = [w3[m] * near[m] for m in range(6)]
        new = ((s3[...] + terms[0]) + (terms[1] + terms[2])) + ((terms[3] + terms[4]) + terms[5])
        return jnp.where(red3, new, e) if red else jnp.where(red3, e, new)

    e = jnp.where(red3, scaled3, 0.0)
    e = sweep3(e, False)
    e = lax.fori_loop(0, CSWEEPS - 1, lambda _, e: sweep3(sweep3(e, True), False), e)

    wide3 = matmul(e.reshape(px * y3, 128), pmat[...]).reshape(px, y3, 256)
    for h in (0, 1):
        part = wide3[:, :, h * 128 : (h + 1) * 128]
        for i in range(px):
            up2[h * px + i, pl.ds(0, y3, 2), :] = part[i]
            up2[h * px + i, pl.ds(1, y3, 2), :] = part[i]

    @pl.loop(0, gx // 2)
    def _(i):
        add = up2[i]
        for j in (1, 2):
            v2[2 * i + j, 8 : 8 + gy, :] = v2[2 * i + j, 8 : 8 + gy, :] + add

    half_sweep(v2, w2, s2, gy, gx, 4, True)
    half_sweep(v2, w2, s2, gy, gx, 4, False)

    def prolong(coarse, vpad, up, count, rows):
        planes, crows, cols = coarse.shape
        flat = coarse.reshape(planes * crows, cols)
        span = (rows + 16) // 2
        for c in range(cols // 128):
            got = matmul(flat[:, c * 128 : (c + 1) * 128], pmat[...])
            got = got.reshape(planes, crows, 256)
            for i in range(planes):
                for q in (0, 1):
                    part = got[i, 4 : 4 + span, q * 128 : (q + 1) * 128]
                    up[i, 2 * c + q, pl.ds(0, span, 2), :] = part
                    up[i, 2 * c + q, pl.ds(1, span, 2), :] = part

        for p in range(count + 2):
            for c in range(cols // 64):
                lanes = pl.ds(c * 128, 128)
                vpad[p, :, lanes] = vpad[p, :, lanes] + up[(p + 1) // 2, c]

    rows2 = pl.ds(pl.multiple_of(n * y2, 8), y2 + 16)
    prolong(v2[pl.ds(w * x2, x2 + 2), rows2, :], v1, up1, x1, y1)
    half_sweep(v1, w1, s1, y1, x1, x1, True)
    halo_start(V1C, 1, pad=v1)
    halo_finish(V1C, 1, v1)
    half_sweep(v1, w1, s1, y1, x1, x1, False)
    halo_start(V1D, 1, pad=v1)
    halo_finish(V1D, 1, v1)

    prolong(v1[...], v0, up0, x0, y0)
    half_sweep(v0, w0, s0, y0, x0, 1, True)
    halo_start(V0C, 0, pad=v0)
    halo_finish(V0C, 0, v0)
    half_sweep(v0, w0, s0, y0, x0, 1, False, out=out_ref)


def solution(mesh):
    wn, nn = mesh.shape["wide"], mesh.shape["narrow"]
    placed = P("wide", "narrow", None)

    def on_device(sources, permeability):
        x0, y0, z0 = sources.shape
        x1, y1, z1 = x0 // 2, y0 // 2, z0 // 2
        x2, y2, z2 = x1 // 2, y1 // 2, z1 // 2
        gx, gy = x2 * wn, y2 * nn
        px, y3 = gx // 4, gy // 2
        pad0, pad1, pad2 = (x0 + 2, y0 + 16, z0), (x1 + 2, y1 + 16, z1), (gx + 2, gy + 16, z2)
        l0, l1, l2 = (x0, y0, z0), (x1, y1, z1), (gx, gy, z2)
        v = lambda *shape: pltpu.VMEM(shape, F32)
        scratch = [
            v(*pad0), v(*pad0), v(6, *l0), v(*l0), v(*l0),
            v(*pad1), v(*pad1), v(6, *l1), v(*l1), v(*l1), v(*l1), v(*l1),
            v(*pad2), v(*pad2), v(6, *l2), v(*l2), v(*l2), v(*l2), v(x2, y2, z2), v(x2, y2, z2),
            v(wn, nn, x2, y2, z2), v(wn, nn, x2, y2, z2),
            v(6, px, y3, 128), v(px, y3, 128),
            v(2, z0 // 128, max(y0, gy), 128), v(x1, y1, z0), v(x2, y2, z1), v(px, y3, 256),
            v(x1 + 2, z0 // 128, y0 + 16, 128), v(x2 + 2, z1 // 128, y1 + 16, 128), v(gx // 2, gy, z2),
            v(256, 128), v(128, 256),
            v(4, 2, y0, z0), v(4, 2, y0, z0), v(4, 2, 8, z0), v(4, 2, 8, z0),
            v(5, 2, y1, z1), v(5, 2, y1, z1), v(5, 2, 8, z1), v(5, 2, 8, z1),
            pltpu.SemaphoreType.DMA((9, 4)), pltpu.SemaphoreType.DMA((9, 4)),
            pltpu.SemaphoreType.DMA((2, wn - 1)), pltpu.SemaphoreType.DMA((2, wn - 1)),
            pltpu.SemaphoreType.DMA((2, nn - 1)), pltpu.SemaphoreType.DMA((2, nn - 1)),
        ]
        return pl.pallas_call(
            functools.partial(kernel, (wn, nn)),
            out_shape=jax.ShapeDtypeStruct(sources.shape, F32),
            in_specs=[pl.BlockSpec(memory_space=pltpu.VMEM)] * 2,
            out_specs=pl.BlockSpec(memory_space=pltpu.VMEM),
            scratch_shapes=scratch,
            compiler_params=pltpu.CompilerParams(
                collective_id=0, has_side_effects=True, vmem_limit_bytes=60 * 1024 * 1024
            ),
        )(sources, permeability)

    return jax.shard_map(
        on_device, mesh=mesh, in_specs=(placed, placed), out_specs=placed, check_vma=False
    )
```

```python
import functools

import jax
import jax.numpy as jnp
from jax import lax
from jax.experimental import pallas as pl
from jax.experimental.pallas import tpu as pltpu
from jax.sharding import PartitionSpec as P

CSWEEPS = 16
F32 = jnp.float32
MESH = pl.DeviceIdType.MESH
K0, V0A, V0B, V0C, K1, V1A, V1B, V1C, V1D = range(9)


def iota(shape, dim):
    return lax.broadcasted_iota(jnp.int32, shape, dim)


def red_cells(shape, plane):
    total = iota(shape, 0) + iota(shape, 1) + plane
    return (total & 1) == 0


def matmul(left, right):
    return jnp.dot(left, right, precision=lax.Precision.HIGHEST, preferred_element_type=F32)


def each_plane(count, step, body, part="all"):
    if part == "edge":
        body(0)
        body(count - 1)
        return
    low, high = (1, count - 1) if part == "inner" else (0, count)
    if high - low == step:
        for i in range(low, high):
            body(i)
        return

    @pl.loop(0, (high - low) // step)
    def _(chunk):
        for i in range(step):
            body(low + chunk * step + i)


def shift(array, amount, axis):
    return pltpu.roll(array, amount % array.shape[axis], axis)


def coefficients(kpad, weights, diag, scaled, right, square, rows, count, step, part="all"):
    def body(i):
        k = kpad[i + 1, 8 : 8 + rows, :]
        lane = iota(k.shape, 1)
        last = k.shape[1] - 1
        up = jnp.where(lane == last, 0.0, shift(k, -1, 1))
        down = jnp.where(lane == 0, 0.0, shift(k, 1, 1))
        faces = [
            kpad[i + 2, 8 : 8 + rows, :],
            kpad[i, 8 : 8 + rows, :],
            kpad[i + 1, 9 : 9 + rows, :],
            kpad[i + 1, 7 : 7 + rows, :],
            up,
            down,
        ]
        faces = [0.5 * (k + face) for face in faces]
        total = functools.reduce(lambda a, b: a + b, faces)
        inverse = 1.0 / total
        for n, face in enumerate(faces):
            w = face * inverse
            if n == 4:
                w = jnp.where(lane == last, 0.0, w)
            if n == 5:
                w = jnp.where(lane == 0, 0.0, w)
            weights[n, i] = w
        diag[i] = total * (1.0 / square)
        if right is not None:
            scaled[i] = (square * inverse) * right[i]
        else:
            scaled[i] = square * inverse

    each_plane(count, step, body, part)


def updated(vpad, weights, scaled, i, rows):
    v = vpad[i + 1, 8 : 8 + rows, :]
    a = weights[0, i] * vpad[i + 2, 8 : 8 + rows, :] + weights[1, i] * vpad[i, 8 : 8 + rows, :]
    b = (
        weights[2, i] * vpad[i + 1, 9 : 9 + rows, :]
        + weights[3, i] * vpad[i + 1, 7 : 7 + rows, :]
    )
    c = weights[4, i] * shift(v, -1, 1) + weights[5, i] * shift(v, 1, 1)
    return v, (scaled[i] + a) + (b + c)


def first_red(vpad, scaled, rows, count, step, part="all"):
    def body(i):
        s = scaled[i]
        vpad[i + 1, 8 : 8 + rows, :] = jnp.where(red_cells(s.shape, i), s, 0.0)

    each_plane(count, step, body, part)


def half_sweep(vpad, weights, scaled, rows, count, step, red, out=None, part="all"):
    def body(i):
        v, new = updated(vpad, weights, scaled, i, rows)
        cells = red_cells(v.shape, i)
        value = jnp.where(cells, new, v) if red else jnp.where(cells, v, new)
        if out is None:
            vpad[i + 1, 8 : 8 + rows, :] = value
        else:
            out[i] = value

    each_plane(count, step, body, part)


def restrict_pair(first, second, tmp, slot):
    half = first.shape[0] // 2
    total = first + second
    parts = []
    for c in range(first.shape[1] // 128):
        tmp[slot, c, : 2 * half, :] = total[:, c * 128 : (c + 1) * 128]
        parts.append(tmp[slot, c, pl.ds(0, half, 2), :] + tmp[slot, c, pl.ds(1, half, 2), :])
    return parts


def kernel(sizes, b_hbm, k_hbm, out_hbm, *s):
    wn, nn = sizes
    (kp0, v0, w0, d0, s0, kp1, v1, w1, d1, s1, b1, k1, kp2, v2, w2, d2, s2, f2, b2l, k2l,
     gk, gb, w3, s3, tmp, half0, half1, half2, up0, up1, up2, rmat, pmat,
     ws0, wr0, ns0, nr0, ws1, wr1, ns1, nr1,
     hs, hr, gsa, gra, gsb, grb, b_ref, out_ref, ls) = s
    x0, y0, z0 = b_hbm.shape
    half_y0 = y0 // 2
    x1, y1, z1 = x0 // 2, y0 // 2, z0 // 2
    x2, y2, z2 = x1 // 2, y1 // 2, z1 // 2
    gx, gy = x2 * wn, y2 * nn
    px = gx // 4
    y3 = gy // 2
    w, n = lax.axis_index("wide"), lax.axis_index("narrow")

    def wide(d):
        return (lax.rem(w + d, wn), n)

    def narrow(d):
        return (w, lax.rem(n + d, nn))

    barrier = pltpu.get_barrier_semaphore()
    for d in range(1, wn):
        pl.semaphore_signal(barrier, inc=1, device_id=wide(d), device_id_type=MESH)
    for d in range(1, nn):
        pl.semaphore_signal(barrier, inc=1, device_id=narrow(d), device_id_type=MESH)

    inside = pl.ds(8, y0)
    k_in = pltpu.make_async_copy(k_hbm, kp0.at[pl.ds(1, x0), inside, :], ls.at[0])
    k_in.start()
    b_in = pltpu.make_async_copy(b_hbm, b_ref, ls.at[1])
    b_in.start()

    @pl.when(w == 0)
    def _():
        kp0[0] = jnp.zeros(kp0.shape[1:], F32)

    @pl.when(w == wn - 1)
    def _():
        kp0[x0 + 1] = jnp.zeros(kp0.shape[1:], F32)

    rmat[...] = jnp.where(iota((256, 128), 0) // 2 == iota((256, 128), 1), 1.0, 0.0)
    pmat[...] = jnp.where(iota((128, 256), 0) == iota((128, 256), 1) // 2, 1.0, 0.0)

    def clear(pad, rows, ends=True):
        planes = pad.shape[0]
        zero = jnp.zeros(pad.shape[1:], F32)
        strip = jnp.zeros((8, pad.shape[2]), F32)
        if ends:
            pad[0] = zero
            pad[planes - 1] = zero

        @pl.loop(1, planes - 1)
        def _(i):
            pad[i, 0:8, :] = strip
            pad[i, 8 + rows : 16 + rows, :] = strip

    def buffers(rnd, level):
        if level == 0:
            return (ws0, wr0, ns0, nr0, rnd, x0, y0)
        return (ws1, wr1, ns1, nr1, rnd - K1, x1, y1)

    def wide_copies(rnd, level):
        ws, wr, _, _, r, _, _ = buffers(rnd, level)
        specs = []
        for side in (0, 1):
            if rnd == K0:
                src = k_hbm.at[(0, x0 - 1)[side]]
                dst = kp0.at[(x0 + 1, 0)[side], inside, :]
            else:
                src, dst = ws.at[r, side], wr.at[r, 1 - side]
            specs.append((
                w > 0 if side == 0 else w < wn - 1,
                w < wn - 1 if side == 0 else w > 0,
                pltpu.make_async_remote_copy(
                    src_ref=src, dst_ref=dst,
                    send_sem=hs.at[rnd, side], recv_sem=hr.at[rnd, side],
                    device_id=wide(wn - 1 if side == 0 else 1), device_id_type=MESH),
            ))
        return specs

    def narrow_copies(rnd, level):
        _, _, ns, nr, r, _, _ = buffers(rnd, level)
        specs = []
        for side in (0, 1):
            specs.append((
                n > 0 if side == 0 else n < nn - 1,
                n < nn - 1 if side == 0 else n > 0,
                pltpu.make_async_remote_copy(
                    src_ref=ns.at[r, side], dst_ref=nr.at[r, 1 - side],
                    send_sem=hs.at[rnd, 2 + side], recv_sem=hr.at[rnd, 2 + side],
                    device_id=narrow(nn - 1 if side == 0 else 1), device_id_type=MESH),
            ))
        return specs

    def start_all(specs):
        for sends, _, copy in specs:
            @pl.when(sends)
            def _(copy=copy):
                copy.start()

    def finish_all(specs):
        for sends, receives, copy in specs:
            @pl.when(receives)
            def _(copy=copy):
                copy.wait_recv()

            @pl.when(sends)
            def _(copy=copy):
                copy.wait_send()

    def colour_of(rnd, plane):
        cells = red_cells((half_y0, z0), plane)
        return jnp.logical_not(cells) if rnd == V0B else cells

    def start_wide(rnd, level, pad):
        ws, _, _, _, r, count, rows = buffers(rnd, level)
        if rnd != K0:
            for side, i in ((0, 0), (1, count - 1)):
                face = pad[i + 1, 8 : 8 + rows, :]
                if level == 0:
                    cells = colour_of(rnd, i)
                    face = jnp.where(cells, face[:half_y0], shift(face[half_y0:], 1, 1))
                ws[r, side] = face
        start_all(wide_copies(rnd, level))

    def start_narrow(rnd, level, pad):
        _, _, ns, _, r, count, rows = buffers(rnd, level)
        for i in range(count):
            ns[r, 0, i : i + 1, :] = pad[i + 1, 8:9, :]
            ns[r, 1, i : i + 1, :] = pad[i + 1, 7 + rows : 8 + rows, :]
        start_all(narrow_copies(rnd, level))

    def finish_wide(rnd, level, pad):
        _, wr, _, _, r, count, rows = buffers(rnd, level)
        finish_all(wide_copies(rnd, level))
        if rnd == K0:
            return
        for side, i in ((0, -1), (1, count)):
            @pl.when(w > 0 if side == 0 else w < wn - 1)
            def _(side=side, i=i):
                got = wr[r, side]
                if level == 0:
                    cells = colour_of(rnd, i)
                    upper, lower = pl.ds(8, half_y0), pl.ds(8 + half_y0, half_y0)
                    pad[i + 1, upper, :] = jnp.where(cells, got, pad[i + 1, upper, :])
                    pad[i + 1, lower, :] = jnp.where(
                        cells, shift(got, -1, 1), pad[i + 1, lower, :]
                    )
                else:
                    pad[i + 1, 8 : 8 + rows, :] = got

    def finish_narrow(rnd, level, pad):
        _, _, _, nr, r, count, rows = buffers(rnd, level)
        finish_all(narrow_copies(rnd, level))

        @pl.when(n > 0)
        def _():
            for i in range(count):
                pad[i + 1, 7:8, :] = nr[r, 0, i : i + 1, :]

        @pl.when(n < nn - 1)
        def _():
            for i in range(count):
                pad[i + 1, 8 + rows : 9 + rows, :] = nr[r, 1, i : i + 1, :]

    def halo_start(rnd, level, pad):
        start_wide(rnd, level, pad)
        start_narrow(rnd, level, pad)

    def halo_finish(rnd, level, pad):
        finish_narrow(rnd, level, pad)
        finish_wide(rnd, level, pad)

    pl.semaphore_wait(barrier, wn - 1 + nn - 1)
    start_wide(K0, 0, kp0)
    k_in.wait()
    start_narrow(K0, 0, kp0)

    def gather_wide(g, which, local):
        copies = []
        for d in range(1, wn):
            copies.append(pltpu.make_async_remote_copy(
                src_ref=local, dst_ref=g.at[w, n],
                send_sem=gsa.at[which, d - 1], recv_sem=gra.at[which, d - 1],
                device_id=wide(d), device_id_type=MESH))
        return copies

    near_first = sorted(range(1, wn), key=lambda d: min(d, wn - d))

    def relay_copies(g, which, d, local):
        at = lax.rem(w + wn - d, wn)
        return [
            pltpu.make_async_remote_copy(
                src_ref=local if d == 0 else g.at[at, n], dst_ref=g.at[at, n],
                send_sem=gsb.at[which, d, e - 1], recv_sem=grb.at[which, d, e - 1],
                device_id=narrow(e), device_id_type=MESH)
            for e in range(1, nn)
        ]

    def gather_start(g, which, local):
        for copy in gather_wide(g, which, local)[::-1]:
            copy.start()
        for copy in relay_copies(g, which, 0, local):
            copy.start()

    def gather_relay(g, which, local):
        arriving = gather_wide(g, which, local)
        for d in near_first:
            arriving[d - 1].wait_recv()
            for copy in relay_copies(g, which, d, local):
                copy.start()

    def gather_finish(g, which, local):
        for d in [0] + near_first:
            for copy in relay_copies(g, which, d, local):
                copy.wait_recv()
        for d in [0] + near_first:
            for copy in relay_copies(g, which, d, local):
                copy.wait_send()
        for copy in gather_wide(g, which, local):
            copy.wait_send()

    for i in range(x1):
        for c, part in enumerate(restrict_pair(kp0[2 * i + 1, inside, :], kp0[2 * i + 2, inside, :], tmp, i % 2)):
            half0[i, :, pl.ds(c * 128, 128)] = part

    def lanes_down(half, store, planes, rows, cols):
        flat = half[...].reshape(planes * rows, cols)
        for c in range(cols // 256):
            got = matmul(flat[:, c * 256 : (c + 1) * 256], rmat[...]) * 0.125
            store(c, got.reshape(planes, rows, 128))

    def store_k1(c, got):
        k1[:, :, pl.ds(c * 128, 128)] = got
        kp1[1 : 1 + x1, 8 : 8 + y1, pl.ds(c * 128, 128)] = got

    lanes_down(half0, store_k1, x1, y1, z0)
    halo_start(K1, 1, pad=kp1)
    for i in range(x2):
        for c, part in enumerate(restrict_pair(k1[2 * i], k1[2 * i + 1], tmp, i % 2)):
            half1[i, :, pl.ds(c * 128, 128)] = part

    def store_k2(c, got):
        k2l[...] = got
        gk[w, n] = got

    lanes_down(half1, store_k2, x2, y2, z1)
    gather_start(gk, 0, k2l)
    clear(kp0, y0, ends=False)
    for pad, rows in ((v0, y0), (kp1, y1), (v1, y1), (kp2, gy), (v2, gy)):
        clear(pad, rows)

    b_in.wait()
    finish_narrow(K0, 0, kp0)
    finish_wide(K0, 0, kp0)
    level0 = (y0, x0, 2)
    for part in ("edge", "inner"):
        coefficients(kp0, w0, d0, s0, b_ref, 1.0, *level0, part=part)
        first_red(v0, s0, *level0, part=part)
        if part == "edge":
            start_wide(V0A, 0, v0)
    start_narrow(V0A, 0, v0)
    halo_finish(K1, 1, kp1)
    coefficients(kp1, w1, d1, s1, None, 4.0, y1, x1, x1)
    halo_finish(V0A, 0, v0)
    half_sweep(v0, w0, s0, *level0, False, part="edge")
    start_wide(V0B, 0, v0)
    half_sweep(v0, w0, s0, *level0, False, part="inner")
    start_narrow(V0B, 0, v0)
    gather_relay(gk, 0, k2l)
    finish_narrow(V0B, 0, v0)

    def residual(vpad, weights, scaled, diag, i, rows):
        v, new = updated(vpad, weights, scaled, i, rows)
        return diag[i] * (new - v)

    def restrict0(i, slot):
        first = residual(v0, w0, s0, d0, 2 * i, y0)
        second = residual(v0, w0, s0, d0, 2 * i + 1, y0)
        for c, part in enumerate(restrict_pair(first, second, tmp, slot)):
            half0[i, :, pl.ds(c * 128, 128)] = part

    @pl.loop(1, x1 - 1)
    def _(i):
        restrict0(i, 0)

    finish_wide(V0B, 0, v0)
    restrict0(0, 0)
    restrict0(x1 - 1, 1)

    def store_b1(c, got):
        b1[:, :, pl.ds(c * 128, 128)] = got

    lanes_down(half0, store_b1, x1, y1, z0)

    for i in range(x1):
        s1[i] = s1[i] * b1[i]
    first_red(v1, s1, y1, x1, x1)
    halo_start(V1A, 1, pad=v1)
    halo_finish(V1A, 1, v1)
    half_sweep(v1, w1, s1, y1, x1, x1, False)
    halo_start(V1B, 1, pad=v1)
    gather_finish(gk, 0, k2l)
    for a in range(wn):
        for c in range(nn):
            kp2[1 + a * x2 : 1 + (a + 1) * x2, 8 + c * y2 : 8 + (c + 1) * y2, :] = gk[a, c]
    halo_finish(V1B, 1, v1)
    for i in range(x2):
        first = residual(v1, w1, s1, d1, 2 * i, y1)
        second = residual(v1, w1, s1, d1, 2 * i + 1, y1)
        for c, part in enumerate(restrict_pair(first, second, tmp, i % 2)):
            half1[i, :, pl.ds(c * 128, 128)] = part

    def store_b2(c, got):
        b2l[...] = got
        gb[w, n] = got

    lanes_down(half1, store_b2, x2, y2, z1)
    gather_start(gb, 1, b2l)

    coefficients(kp2, w2, d2, f2, None, 16.0, gy, gx, 4)

    def pack_down(get, tag):
        @pl.loop(0, px)
        def _(i):
            for h in (0, 1):
                part = restrict_pair(*get(i + h * px), tmp, h)[0]
                half2[i, :, pl.ds(h * 128, 128)] = part

        return matmul(half2[...].reshape(px * y3, 256), rmat[...]).reshape(px, y3, 128) * 0.125

    def plane_of(i):
        return kp2[1 + 2 * i, 8 : 8 + gy, :], kp2[2 + 2 * i, 8 : 8 + gy, :]

    k3 = pack_down(plane_of, 0)
    shape3 = (px, y3, 128)
    p_at, r_at, l_at = iota(shape3, 0), iota(shape3, 1), iota(shape3, 2)
    z_at = l_at & 63
    outside = [
        (p_at == px - 1) & (l_at >= 64),
        (p_at == 0) & (l_at < 64),
        r_at == y3 - 1,
        r_at == 0,
        z_at == 63,
        z_at == 0,
    ]

    def neighbours(v):
        xp = jnp.concatenate([v[1:], shift(v[:1], 64, 2)], axis=0)
        xm = jnp.concatenate([shift(v[-1:], 64, 2), v[:-1]], axis=0)
        return [xp, xm, shift(v, -1, 1), shift(v, 1, 1), shift(v, -1, 2), shift(v, 1, 2)]

    faces3 = [
        0.5 * (k3 + jnp.where(out, 0.0, near)) for out, near in zip(outside, neighbours(k3))
    ]
    total3 = functools.reduce(lambda a, b: a + b, faces3)
    inverse3 = 1.0 / total3
    for m in range(6):
        w3[m] = jnp.where(outside[m], 0.0, faces3[m] * inverse3)
    s3[...] = 64.0 * inverse3

    gather_relay(gb, 1, b2l)
    gather_finish(gb, 1, b2l)

    for a in range(wn):
        for c in range(nn):
            for i in range(x2):
                rows = pl.ds(c * y2, y2)
                s2[a * x2 + i, rows, :] = f2[a * x2 + i, rows, :] * gb[a, c, i]
    first_red(v2, s2, gy, gx, 4)
    half_sweep(v2, w2, s2, gy, gx, 4, False)

    def resid2(i):
        return (residual(v2, w2, s2, d2, 2 * i, gy), residual(v2, w2, s2, d2, 2 * i + 1, gy))

    b3 = pack_down(resid2, 1)
    scaled3 = s3[...] * b3
    s3[...] = scaled3
    first_at = p_at + jnp.where(l_at >= 64, px, 0)
    red3 = ((first_at + r_at + z_at) & 1) == 0

    def sweep3(e, red):
        near = neighbours(e)
        terms = [w3[m] * near[m] for m in range(6)]
        new = ((s3[...] + terms[0]) + (terms[1] + terms[2])) + ((terms[3] + terms[4]) + terms[5])
        return jnp.where(red3, new, e) if red else jnp.where(red3, e, new)

    e = jnp.where(red3, scaled3, 0.0)
    e = sweep3(e, False)
    e = lax.fori_loop(0, CSWEEPS - 1, lambda _, e: sweep3(sweep3(e, True), False), e)

    wide3 = matmul(e.reshape(px * y3, 128), pmat[...]).reshape(px, y3, 256)
    for h in (0, 1):
        part = wide3[:, :, h * 128 : (h + 1) * 128]
        for i in range(px):
            up2[h * px + i, pl.ds(0, y3, 2), :] = part[i]
            up2[h * px + i, pl.ds(1, y3, 2), :] = part[i]

    @pl.loop(0, gx // 2)
    def _(i):
        add = up2[i]
        for j in (1, 2):
            v2[2 * i + j, 8 : 8 + gy, :] = v2[2 * i + j, 8 : 8 + gy, :] + add

    half_sweep(v2, w2, s2, gy, gx, 4, True)
    half_sweep(v2, w2, s2, gy, gx, 4, False)

    def prolong(coarse, vpad, up, count, rows):
        planes, crows, cols = coarse.shape
        flat = coarse.reshape(planes * crows, cols)
        span = (rows + 16) // 2
        for c in range(cols // 128):
            got = matmul(flat[:, c * 128 : (c + 1) * 128], pmat[...])
            got = got.reshape(planes, crows, 256)
            for i in range(planes):
                for q in (0, 1):
                    part = got[i, 4 : 4 + span, q * 128 : (q + 1) * 128]
                    up[i, 2 * c + q, pl.ds(0, span, 2), :] = part
                    up[i, 2 * c + q, pl.ds(1, span, 2), :] = part

        for p in range(count + 2):
            for c in range(cols // 64):
                lanes = pl.ds(c * 128, 128)
                vpad[p, :, lanes] = vpad[p, :, lanes] + up[(p + 1) // 2, c]

    rows2 = pl.ds(pl.multiple_of(n * y2, 8), y2 + 16)
    prolong(v2[pl.ds(w * x2, x2 + 2), rows2, :], v1, up1, x1, y1)
    half_sweep(v1, w1, s1, y1, x1, x1, True)
    halo_start(V1C, 1, pad=v1)
    halo_finish(V1C, 1, v1)
    half_sweep(v1, w1, s1, y1, x1, x1, False)
    halo_start(V1D, 1, pad=v1)
    halo_finish(V1D, 1, v1)

    prolong(v1[...], v0, up0, x0, y0)
    half_sweep(v0, w0, s0, *level0, True, part="edge")
    start_wide(V0C, 0, v0)
    half_sweep(v0, w0, s0, *level0, True, part="inner")
    start_narrow(V0C, 0, v0)
    finish_narrow(V0C, 0, v0)
    half_sweep(v0, w0, s0, *level0, False, out=out_ref, part="inner")
    results = [
        pltpu.make_async_copy(out_ref.at[planes], out_hbm.at[planes], ls.at[2 + m])
        for m, planes in enumerate((pl.ds(1, x0 - 2), pl.ds(0, 1), pl.ds(x0 - 1, 1)))
    ]
    results[0].start()
    finish_wide(V0C, 0, v0)
    half_sweep(v0, w0, s0, *level0, False, out=out_ref, part="edge")
    results[1].start()
    results[2].start()
    for copy in results:
        copy.wait()


def solution(mesh):
    wn, nn = mesh.shape["wide"], mesh.shape["narrow"]
    placed = P("wide", "narrow", None)

    def on_device(sources, permeability):
        x0, y0, z0 = sources.shape
        x1, y1, z1 = x0 // 2, y0 // 2, z0 // 2
        x2, y2, z2 = x1 // 2, y1 // 2, z1 // 2
        gx, gy = x2 * wn, y2 * nn
        px, y3 = gx // 4, gy // 2
        pad0, pad1, pad2 = (x0 + 2, y0 + 16, z0), (x1 + 2, y1 + 16, z1), (gx + 2, gy + 16, z2)
        l0, l1, l2 = (x0, y0, z0), (x1, y1, z1), (gx, gy, z2)
        v = lambda *shape: pltpu.VMEM(shape, F32)
        scratch = [
            v(*pad0), v(*pad0), v(6, *l0), v(*l0), v(*l0),
            v(*pad1), v(*pad1), v(6, *l1), v(*l1), v(*l1), v(*l1), v(*l1),
            v(*pad2), v(*pad2), v(6, *l2), v(*l2), v(*l2), v(*l2), v(x2, y2, z2), v(x2, y2, z2),
            v(wn, nn, x2, y2, z2), v(wn, nn, x2, y2, z2),
            v(6, px, y3, 128), v(px, y3, 128),
            v(2, z0 // 128, max(y0, gy), 128), v(x1, y1, z0), v(x2, y2, z1), v(px, y3, 256),
            v(x1 + 2, z0 // 128, y0 + 16, 128), v(x2 + 2, z1 // 128, y1 + 16, 128), v(gx // 2, gy, z2),
            v(256, 128), v(128, 256),
            v(4, 2, y0 // 2, z0), v(4, 2, y0 // 2, z0), v(4, 2, 8, z0), v(4, 2, 8, z0),
            v(5, 2, y1, z1), v(5, 2, y1, z1), v(5, 2, 8, z1), v(5, 2, 8, z1),
            pltpu.SemaphoreType.DMA((9, 4)), pltpu.SemaphoreType.DMA((9, 4)),
            pltpu.SemaphoreType.DMA((2, wn - 1)), pltpu.SemaphoreType.DMA((2, wn - 1)),
            pltpu.SemaphoreType.DMA((2, wn, nn - 1)), pltpu.SemaphoreType.DMA((2, wn, nn - 1)),
            v(*l0), v(*l0), pltpu.SemaphoreType.DMA((5,)),
        ]
        return pl.pallas_call(
            functools.partial(kernel, (wn, nn)),
            out_shape=jax.ShapeDtypeStruct(sources.shape, F32),
            in_specs=[pl.BlockSpec(memory_space=pltpu.HBM)] * 2,
            out_specs=pl.BlockSpec(memory_space=pltpu.HBM),
            scratch_shapes=scratch,
            compiler_params=pltpu.CompilerParams(
                collective_id=0, has_side_effects=True, vmem_limit_bytes=60 * 1024 * 1024
            ),
        )(sources, permeability)

    return jax.shard_map(
        on_device, mesh=mesh, in_specs=(placed, placed), out_specs=placed, check_vma=False
    )
```

```python
import functools

import jax
import jax.numpy as jnp
from jax import lax
from jax.experimental import pallas as pl
from jax.experimental.pallas import tpu as pltpu
from jax.sharding import PartitionSpec as P

CSWEEPS = 16
F32 = jnp.float32
MESH = pl.DeviceIdType.MESH
K0, V0A, V0B, V0C = range(4)
K1, S1, V1 = range(3)


def iota(shape, dim):
    return lax.broadcasted_iota(jnp.int32, shape, dim)


def red_cells(shape, plane):
    total = iota(shape, 0) + iota(shape, 1) + plane
    return (total & 1) == 0


def matmul(left, right):
    return jnp.dot(left, right, precision=lax.Precision.HIGHEST, preferred_element_type=F32)


def each_plane(count, step, body, part="all"):
    if part == "edge":
        body(0)
        body(count - 1)
        return
    low, high = (1, count - 1) if part == "inner" else (0, count)
    if high - low == step:
        for i in range(low, high):
            body(i)
        return

    @pl.loop(0, (high - low) // step)
    def _(chunk):
        for i in range(step):
            body(low + chunk * step + i)


def shift(array, amount, axis):
    return pltpu.roll(array, amount % array.shape[axis], axis)


def coefficients(kpad, weights, diag, scaled, right, square, rows, count, step, part="all"):
    def body(i):
        k = kpad[i + 1, 8 : 8 + rows, :]
        lane = iota(k.shape, 1)
        last = k.shape[1] - 1
        up = jnp.where(lane == last, 0.0, shift(k, -1, 1))
        down = jnp.where(lane == 0, 0.0, shift(k, 1, 1))
        faces = [
            kpad[i + 2, 8 : 8 + rows, :],
            kpad[i, 8 : 8 + rows, :],
            kpad[i + 1, 9 : 9 + rows, :],
            kpad[i + 1, 7 : 7 + rows, :],
            up,
            down,
        ]
        faces = [0.5 * (k + face) for face in faces]
        total = functools.reduce(lambda a, b: a + b, faces)
        inverse = 1.0 / total
        for n, face in enumerate(faces):
            w = face * inverse
            if n == 4:
                w = jnp.where(lane == last, 0.0, w)
            if n == 5:
                w = jnp.where(lane == 0, 0.0, w)
            weights[n, i] = w
        diag[i] = total * (1.0 / square)
        if right is not None:
            scaled[i] = (square * inverse) * right[i]
        else:
            scaled[i] = square * inverse

    each_plane(count, step, body, part)


def updated(vpad, weights, scaled, i, rows):
    v = vpad[i + 1, 8 : 8 + rows, :]
    a = weights[0, i] * vpad[i + 2, 8 : 8 + rows, :] + weights[1, i] * vpad[i, 8 : 8 + rows, :]
    b = (
        weights[2, i] * vpad[i + 1, 9 : 9 + rows, :]
        + weights[3, i] * vpad[i + 1, 7 : 7 + rows, :]
    )
    c = weights[4, i] * shift(v, -1, 1) + weights[5, i] * shift(v, 1, 1)
    return v, (scaled[i] + a) + (b + c)


def first_red(vpad, scaled, rows, count, step, part="all"):
    def body(i):
        s = scaled[i]
        vpad[i + 1, 8 : 8 + rows, :] = jnp.where(red_cells(s.shape, i), s, 0.0)

    each_plane(count, step, body, part)


def half_sweep(vpad, weights, scaled, rows, count, step, red, out=None, part="all"):
    def body(i):
        v, new = updated(vpad, weights, scaled, i, rows)
        cells = red_cells(v.shape, i)
        value = jnp.where(cells, new, v) if red else jnp.where(cells, v, new)
        if out is None:
            vpad[i + 1, 8 : 8 + rows, :] = value
        else:
            out[i] = value

    each_plane(count, step, body, part)


def restrict_pair(first, second, tmp, slot):
    half = first.shape[0] // 2
    total = first + second
    parts = []
    for c in range(first.shape[1] // 128):
        tmp[slot, c, : 2 * half, :] = total[:, c * 128 : (c + 1) * 128]
        parts.append(tmp[slot, c, pl.ds(0, half, 2), :] + tmp[slot, c, pl.ds(1, half, 2), :])
    return parts


def kernel(sizes, b_hbm, k_hbm, out_hbm, *s):
    wn, nn = sizes
    (kp0, v0, w0, d0, s0, kp1, v1, w1, d1, s1, f1, b1, k1, kp2, v2, w2, d2, s2, f2, b2l, k2l,
     gk, gb, w3, s3, tmp, half0, half1, half2, up0, up1, up2, rmat, pmat,
     ws0, wr0, ns0, nr0, ws1, wr1, ns1, nr1, cs1, cr1,
     hs, hr, hs1, hr1, gsa, gra, gsb, grb, b_ref, out_ref, ls) = s
    x0, y0, z0 = b_hbm.shape
    half_y0 = y0 // 2
    x1, y1, z1 = x0 // 2, y0 // 2, z0 // 2
    x2, y2, z2 = x1 // 2, y1 // 2, z1 // 2
    gx, gy = x2 * wn, y2 * nn
    px = gx // 4
    y3 = gy // 2
    w, n = lax.axis_index("wide"), lax.axis_index("narrow")

    def wide(d):
        return (lax.rem(w + d, wn), n)

    def narrow(d):
        return (w, lax.rem(n + d, nn))

    def diagonal(a, c):
        return (lax.rem(w + (1 if a else wn - 1), wn), lax.rem(n + (1 if c else nn - 1), nn))

    corners = [(a, c) for a in (0, 1) for c in (0, 1)]
    barrier = pltpu.get_barrier_semaphore()
    for a, c in corners:
        pl.semaphore_signal(barrier, inc=1, device_id=diagonal(a, c), device_id_type=MESH)
    for d in range(1, wn):
        pl.semaphore_signal(barrier, inc=1, device_id=wide(d), device_id_type=MESH)
    for d in range(1, nn):
        pl.semaphore_signal(barrier, inc=1, device_id=narrow(d), device_id_type=MESH)

    inside = pl.ds(8, y0)
    k_in = pltpu.make_async_copy(k_hbm, kp0.at[pl.ds(1, x0), inside, :], ls.at[0])
    k_in.start()
    b_in = pltpu.make_async_copy(b_hbm, b_ref, ls.at[1])
    b_in.start()

    @pl.when(w == 0)
    def _():
        kp0[0] = jnp.zeros(kp0.shape[1:], F32)

    @pl.when(w == wn - 1)
    def _():
        kp0[x0 + 1] = jnp.zeros(kp0.shape[1:], F32)

    rmat[...] = jnp.where(iota((256, 128), 0) // 2 == iota((256, 128), 1), 1.0, 0.0)
    pmat[...] = jnp.where(iota((128, 256), 0) == iota((128, 256), 1) // 2, 1.0, 0.0)

    def clear(pad, rows, ends=True):
        planes = pad.shape[0]
        zero = jnp.zeros(pad.shape[1:], F32)
        strip = jnp.zeros((8, pad.shape[2]), F32)
        if ends:
            pad[0] = zero
            pad[planes - 1] = zero

        @pl.loop(1, planes - 1)
        def _(i):
            pad[i, 0:8, :] = strip
            pad[i, 8 + rows : 16 + rows, :] = strip

    def buffers(rnd, level):
        return (ws0, wr0, ns0, nr0, rnd, x0, y0)

    def wide_copies(rnd, level):
        ws, wr, _, _, r, _, _ = buffers(rnd, level)
        specs = []
        for side in (0, 1):
            if rnd == K0:
                src = k_hbm.at[(0, x0 - 1)[side]]
                dst = kp0.at[(x0 + 1, 0)[side], inside, :]
            else:
                src, dst = ws.at[r, side], wr.at[r, 1 - side]
            specs.append((
                w > 0 if side == 0 else w < wn - 1,
                w < wn - 1 if side == 0 else w > 0,
                pltpu.make_async_remote_copy(
                    src_ref=src, dst_ref=dst,
                    send_sem=hs.at[rnd, side], recv_sem=hr.at[rnd, side],
                    device_id=wide(wn - 1 if side == 0 else 1), device_id_type=MESH),
            ))
        return specs

    def narrow_copies(rnd, level):
        _, _, ns, nr, r, _, _ = buffers(rnd, level)
        specs = []
        for side in (0, 1):
            specs.append((
                n > 0 if side == 0 else n < nn - 1,
                n < nn - 1 if side == 0 else n > 0,
                pltpu.make_async_remote_copy(
                    src_ref=ns.at[r, side], dst_ref=nr.at[r, 1 - side],
                    send_sem=hs.at[rnd, 2 + side], recv_sem=hr.at[rnd, 2 + side],
                    device_id=narrow(nn - 1 if side == 0 else 1), device_id_type=MESH),
            ))
        return specs

    def start_all(specs):
        for sends, _, copy in specs:
            @pl.when(sends)
            def _(copy=copy):
                copy.start()

    def finish_all(specs):
        for sends, receives, copy in specs:
            @pl.when(receives)
            def _(copy=copy):
                copy.wait_recv()

            @pl.when(sends)
            def _(copy=copy):
                copy.wait_send()

    def colour_of(rnd, plane):
        cells = red_cells((half_y0, z0), plane)
        return jnp.logical_not(cells) if rnd == V0B else cells

    def start_wide(rnd, level, pad):
        ws, _, _, _, r, count, rows = buffers(rnd, level)
        if rnd != K0:
            for side, i in ((0, 0), (1, count - 1)):
                face = pad[i + 1, 8 : 8 + rows, :]
                if level == 0:
                    cells = colour_of(rnd, i)
                    face = jnp.where(cells, face[:half_y0], shift(face[half_y0:], 1, 1))
                ws[r, side] = face
        start_all(wide_copies(rnd, level))

    def start_narrow(rnd, level, pad):
        _, _, ns, _, r, count, rows = buffers(rnd, level)
        for i in range(count):
            ns[r, 0, i : i + 1, :] = pad[i + 1, 8:9, :]
            ns[r, 1, i : i + 1, :] = pad[i + 1, 7 + rows : 8 + rows, :]
        start_all(narrow_copies(rnd, level))

    def finish_wide(rnd, level, pad):
        _, wr, _, _, r, count, rows = buffers(rnd, level)
        finish_all(wide_copies(rnd, level))
        if rnd == K0:
            return
        for side, i in ((0, -1), (1, count)):
            @pl.when(w > 0 if side == 0 else w < wn - 1)
            def _(side=side, i=i):
                got = wr[r, side]
                if level == 0:
                    cells = colour_of(rnd, i)
                    upper, lower = pl.ds(8, half_y0), pl.ds(8 + half_y0, half_y0)
                    pad[i + 1, upper, :] = jnp.where(cells, got, pad[i + 1, upper, :])
                    pad[i + 1, lower, :] = jnp.where(
                        cells, shift(got, -1, 1), pad[i + 1, lower, :]
                    )
                else:
                    pad[i + 1, 8 : 8 + rows, :] = got

    def finish_narrow(rnd, level, pad):
        _, _, _, nr, r, count, rows = buffers(rnd, level)
        finish_all(narrow_copies(rnd, level))

        @pl.when(n > 0)
        def _():
            for i in range(count):
                pad[i + 1, 7:8, :] = nr[r, 0, i : i + 1, :]

        @pl.when(n < nn - 1)
        def _():
            for i in range(count):
                pad[i + 1, 8 + rows : 9 + rows, :] = nr[r, 1, i : i + 1, :]

    def halo_start(rnd, level, pad):
        start_wide(rnd, level, pad)
        start_narrow(rnd, level, pad)

    def halo_finish(rnd, level, pad):
        finish_narrow(rnd, level, pad)
        finish_wide(rnd, level, pad)

    pl.semaphore_wait(barrier, wn - 1 + nn - 1 + len(corners))
    start_wide(K0, 0, kp0)
    k_in.wait()
    start_narrow(K0, 0, kp0)

    own1 = pl.ds(8, y1)

    def exists(a, c):
        good = None
        for side, at, size in ((a, w, wn), (c, n, nn)):
            if side is not None:
                here = at < size - 1 if side else at > 0
                good = here if good is None else jnp.logical_and(good, here)
        return good

    def copies1(rnd, array):
        specs = []

        def add(slot, a, c, src, dst, target):
            back = [None if side is None else 1 - side for side in (a, c)]
            specs.append((exists(a, c), exists(*back), pltpu.make_async_remote_copy(
                src_ref=src, dst_ref=dst, send_sem=hs1.at[rnd, slot],
                recv_sem=hr1.at[rnd, slot], device_id=target, device_id_type=MESH)))

        for a, c in corners:
            add(4 + 2 * a + c, a, c, cs1.at[rnd, a, c], cr1.at[rnd, 1 - a, 1 - c],
                diagonal(a, c))
        for side in (0, 1):
            if rnd == V1:
                src, dst = ws1.at[side], wr1.at[1 - side]
            else:
                src = array.at[pl.ds((2, x1)[side], 2), own1, :]
                dst = array.at[pl.ds((x1 + 2, 0)[side], 2), own1, :]
            add(side, side, None, src, dst, wide(1 if side else wn - 1))
        for side in (0, 1):
            add(2 + side, None, side, ns1.at[rnd, side], nr1.at[rnd, 1 - side],
                narrow(1 if side else nn - 1))
        return specs

    def start1(rnd, array):
        for a, c in corners:
            row = (8, 7 + y1)[c]
            cs1[rnd, a, c] = array[(2, x1 + 1)[a], row : row + 1, :]
        if rnd == V1:
            ws1[0] = array[2:4, 8 : 8 + y1, :]
            ws1[1] = array[x1 : x1 + 2, 8 : 8 + y1, :]
        for i in range(x1):
            ns1[rnd, 0, 2 * i : 2 * i + 2, :] = array[2 + i, 8:10, :]
            ns1[rnd, 1, 2 * i : 2 * i + 2, :] = array[2 + i, 6 + y1 : 8 + y1, :]
        start_all(copies1(rnd, array))

    def finish1(rnd, array):
        finish_all(copies1(rnd, array)[::-1])
        for side in (0, 1):
            if rnd == V1:
                @pl.when(exists(side, None))
                def _(side=side):
                    at = (0, x1 + 2)[side]
                    array[at : at + 2, 8 : 8 + y1, :] = wr1[side]

            @pl.when(exists(None, side))
            def _(side=side):
                at = (6, 8 + y1)[side]
                for i in range(x1):
                    array[2 + i, at : at + 2, :] = nr1[rnd, side, 2 * i : 2 * i + 2, :]

        for a, c in corners:
            @pl.when(exists(a, c))
            def _(a=a, c=c):
                at = (7, 8 + y1)[c]
                array[(1, x1 + 2)[a], at : at + 1, :] = cr1[rnd, a, c]

    def clear1(array):
        strip = jnp.zeros((8, z1), F32)
        for p in range(x1 + 4):
            array[p, 0:8, :] = strip
            array[p, 8 + y1 :, :] = strip

        for side in (0, 1):
            @pl.when(jnp.logical_not(exists(side, None)))
            def _(side=side):
                at = (0, x1 + 2)[side]
                array[at : at + 2, 8 : 8 + y1, :] = jnp.zeros((2, y1, z1), F32)

    def coefficients1():
        for j in range(1, x1 + 3):
            k = kp1[j]
            lane = iota(k.shape, 1)
            first, last = lane == 0, lane == z1 - 1
            faces = [kp1[j + 1], kp1[j - 1], shift(k, -1, 0), shift(k, 1, 0),
                     jnp.where(last, 0.0, shift(k, -1, 1)), jnp.where(first, 0.0, shift(k, 1, 1))]
            faces = [0.5 * (k + face) for face in faces]
            total = functools.reduce(lambda a, b: a + b, faces)
            inverse = jnp.where(k > 0.0, 1.0 / total, 0.0)
            for m, face in enumerate(faces):
                weight = face * inverse
                if m >= 4:
                    weight = jnp.where(first if m == 5 else last, 0.0, weight)
                w1[m, j] = weight
            d1[j] = total * 0.25
            f1[j] = 4.0 * inverse

    def updated1(j):
        v = v1[j]
        a = w1[0, j] * v1[j + 1] + w1[1, j] * v1[j - 1]
        b = w1[2, j] * shift(v, -1, 0) + w1[3, j] * shift(v, 1, 0)
        c = w1[4, j] * shift(v, -1, 1) + w1[5, j] * shift(v, 1, 1)
        return v, (s1[j] + a) + (b + c)

    def half_sweep1(planes, red):
        for j in planes:
            v, new = updated1(j)
            cells = red_cells(v.shape, j)
            v1[j] = jnp.where(cells, new, v) if red else jnp.where(cells, v, new)

    def gather_wide(g, which, local):
        copies = []
        for d in range(1, wn):
            copies.append(pltpu.make_async_remote_copy(
                src_ref=local, dst_ref=g.at[w, n],
                send_sem=gsa.at[which, d - 1], recv_sem=gra.at[which, d - 1],
                device_id=wide(d), device_id_type=MESH))
        return copies

    near_first = sorted(range(1, wn), key=lambda d: min(d, wn - d))

    def relay_copies(g, which, d, local):
        at = lax.rem(w + wn - d, wn)
        return [
            pltpu.make_async_remote_copy(
                src_ref=local if d == 0 else g.at[at, n], dst_ref=g.at[at, n],
                send_sem=gsb.at[which, d, e - 1], recv_sem=grb.at[which, d, e - 1],
                device_id=narrow(e), device_id_type=MESH)
            for e in range(1, nn)
        ]

    def gather_start(g, which, local):
        for copy in gather_wide(g, which, local)[::-1]:
            copy.start()
        for copy in relay_copies(g, which, 0, local):
            copy.start()

    def gather_relay(g, which, local):
        arriving = gather_wide(g, which, local)
        for d in near_first:
            arriving[d - 1].wait_recv()
            for copy in relay_copies(g, which, d, local):
                copy.start()

    def gather_finish(g, which, local):
        for d in [0] + near_first:
            for copy in relay_copies(g, which, d, local):
                copy.wait_recv()
        for d in [0] + near_first:
            for copy in relay_copies(g, which, d, local):
                copy.wait_send()
        for copy in gather_wide(g, which, local):
            copy.wait_send()

    for i in range(x1):
        for c, part in enumerate(restrict_pair(kp0[2 * i + 1, inside, :], kp0[2 * i + 2, inside, :], tmp, i % 2)):
            half0[i, :, pl.ds(c * 128, 128)] = part

    def lanes_down(half, store, planes, rows, cols):
        flat = half[...].reshape(planes * rows, cols)
        for c in range(cols // 256):
            got = matmul(flat[:, c * 256 : (c + 1) * 256], rmat[...]) * 0.125
            store(c, got.reshape(planes, rows, 128))

    def store_k1(c, got):
        k1[:, :, pl.ds(c * 128, 128)] = got
        kp1[2 : 2 + x1, 8 : 8 + y1, pl.ds(c * 128, 128)] = got

    lanes_down(half0, store_k1, x1, y1, z0)
    clear1(kp1)
    clear1(s1)
    start1(K1, kp1)
    for i in range(x2):
        for c, part in enumerate(restrict_pair(k1[2 * i], k1[2 * i + 1], tmp, i % 2)):
            half1[i, :, pl.ds(c * 128, 128)] = part

    def store_k2(c, got):
        k2l[...] = got
        gk[w, n] = got

    lanes_down(half1, store_k2, x2, y2, z1)
    gather_start(gk, 0, k2l)
    clear(kp0, y0, ends=False)
    for pad, rows in ((v0, y0), (kp2, gy), (v2, gy)):
        clear(pad, rows)

    b_in.wait()
    finish_narrow(K0, 0, kp0)
    finish_wide(K0, 0, kp0)
    level0 = (y0, x0, 2)
    for part in ("edge", "inner"):
        coefficients(kp0, w0, d0, s0, b_ref, 1.0, *level0, part=part)
        first_red(v0, s0, *level0, part=part)
        if part == "edge":
            start_wide(V0A, 0, v0)
    start_narrow(V0A, 0, v0)
    finish1(K1, kp1)
    coefficients1()
    halo_finish(V0A, 0, v0)
    half_sweep(v0, w0, s0, *level0, False, part="edge")
    start_wide(V0B, 0, v0)
    half_sweep(v0, w0, s0, *level0, False, part="inner")
    start_narrow(V0B, 0, v0)
    gather_relay(gk, 0, k2l)
    finish_narrow(V0B, 0, v0)

    def residual(vpad, weights, scaled, diag, i, rows):
        v, new = updated(vpad, weights, scaled, i, rows)
        return diag[i] * (new - v)

    def restrict0(i, slot):
        first = residual(v0, w0, s0, d0, 2 * i, y0)
        second = residual(v0, w0, s0, d0, 2 * i + 1, y0)
        for c, part in enumerate(restrict_pair(first, second, tmp, slot)):
            half0[i, :, pl.ds(c * 128, 128)] = part

    @pl.loop(1, x1 - 1)
    def _(i):
        restrict0(i, 0)

    finish_wide(V0B, 0, v0)
    restrict0(0, 0)
    restrict0(x1 - 1, 1)

    def store_b1(c, got):
        b1[:, :, pl.ds(c * 128, 128)] = got

    lanes_down(half0, store_b1, x1, y1, z0)

    for i in range(x1):
        s1[2 + i, own1, :] = f1[2 + i, own1, :] * b1[i]
    start1(S1, s1)
    gather_finish(gk, 0, k2l)
    for a in range(wn):
        for c in range(nn):
            kp2[1 + a * x2 : 1 + (a + 1) * x2, 8 + c * y2 : 8 + (c + 1) * y2, :] = gk[a, c]
    finish1(S1, s1)
    for j in range(x1 + 4):
        v1[j] = jnp.where(red_cells((y1 + 16, z1), j), s1[j], 0.0)
    half_sweep1(range(1, x1 + 3), False)

    def residual1(i):
        v, new = updated1(2 + i)
        return (d1[2 + i] * (new - v))[8 : 8 + y1]

    for i in range(x2):
        first, second = residual1(2 * i), residual1(2 * i + 1)
        for c, part in enumerate(restrict_pair(first, second, tmp, i % 2)):
            half1[i, :, pl.ds(c * 128, 128)] = part

    def store_b2(c, got):
        b2l[...] = got
        gb[w, n] = got

    lanes_down(half1, store_b2, x2, y2, z1)
    gather_start(gb, 1, b2l)

    coefficients(kp2, w2, d2, f2, None, 16.0, gy, gx, 4)

    def pack_down(get, tag):
        @pl.loop(0, px)
        def _(i):
            for h in (0, 1):
                part = restrict_pair(*get(i + h * px), tmp, h)[0]
                half2[i, :, pl.ds(h * 128, 128)] = part

        return matmul(half2[...].reshape(px * y3, 256), rmat[...]).reshape(px, y3, 128) * 0.125

    def plane_of(i):
        return kp2[1 + 2 * i, 8 : 8 + gy, :], kp2[2 + 2 * i, 8 : 8 + gy, :]

    k3 = pack_down(plane_of, 0)
    shape3 = (px, y3, 128)
    p_at, r_at, l_at = iota(shape3, 0), iota(shape3, 1), iota(shape3, 2)
    z_at = l_at & 63
    outside = [
        (p_at == px - 1) & (l_at >= 64),
        (p_at == 0) & (l_at < 64),
        r_at == y3 - 1,
        r_at == 0,
        z_at == 63,
        z_at == 0,
    ]

    def neighbours(v):
        xp = jnp.concatenate([v[1:], shift(v[:1], 64, 2)], axis=0)
        xm = jnp.concatenate([shift(v[-1:], 64, 2), v[:-1]], axis=0)
        return [xp, xm, shift(v, -1, 1), shift(v, 1, 1), shift(v, -1, 2), shift(v, 1, 2)]

    faces3 = [
        0.5 * (k3 + jnp.where(out, 0.0, near)) for out, near in zip(outside, neighbours(k3))
    ]
    total3 = functools.reduce(lambda a, b: a + b, faces3)
    inverse3 = 1.0 / total3
    for m in range(6):
        w3[m] = jnp.where(outside[m], 0.0, faces3[m] * inverse3)
    s3[...] = 64.0 * inverse3

    gather_relay(gb, 1, b2l)
    gather_finish(gb, 1, b2l)

    for a in range(wn):
        for c in range(nn):
            for i in range(x2):
                rows = pl.ds(c * y2, y2)
                s2[a * x2 + i, rows, :] = f2[a * x2 + i, rows, :] * gb[a, c, i]
    first_red(v2, s2, gy, gx, 4)
    half_sweep(v2, w2, s2, gy, gx, 4, False)

    def resid2(i):
        return (residual(v2, w2, s2, d2, 2 * i, gy), residual(v2, w2, s2, d2, 2 * i + 1, gy))

    b3 = pack_down(resid2, 1)
    scaled3 = s3[...] * b3
    s3[...] = scaled3
    first_at = p_at + jnp.where(l_at >= 64, px, 0)
    red3 = ((first_at + r_at + z_at) & 1) == 0

    def sweep3(e, red):
        near = neighbours(e)
        terms = [w3[m] * near[m] for m in range(6)]
        new = ((s3[...] + terms[0]) + (terms[1] + terms[2])) + ((terms[3] + terms[4]) + terms[5])
        return jnp.where(red3, new, e) if red else jnp.where(red3, e, new)

    e = jnp.where(red3, scaled3, 0.0)
    e = sweep3(e, False)
    e = lax.fori_loop(0, CSWEEPS - 1, lambda _, e: sweep3(sweep3(e, True), False), e)

    wide3 = matmul(e.reshape(px * y3, 128), pmat[...]).reshape(px, y3, 256)
    for h in (0, 1):
        part = wide3[:, :, h * 128 : (h + 1) * 128]
        for i in range(px):
            up2[h * px + i, pl.ds(0, y3, 2), :] = part[i]
            up2[h * px + i, pl.ds(1, y3, 2), :] = part[i]

    @pl.loop(0, gx // 2)
    def _(i):
        add = up2[i]
        for j in (1, 2):
            v2[2 * i + j, 8 : 8 + gy, :] = v2[2 * i + j, 8 : 8 + gy, :] + add

    half_sweep(v2, w2, s2, gy, gx, 4, True)
    half_sweep(v2, w2, s2, gy, gx, 4, False)

    def prolong(coarse, vpad, up, count, rows, depth):
        planes, crows, cols = coarse.shape
        flat = coarse.reshape(planes * crows, cols)
        span = (rows + 16) // 2
        for c in range(cols // 128):
            got = matmul(flat[:, c * 128 : (c + 1) * 128], pmat[...])
            got = got.reshape(planes, crows, 256)
            for i in range(planes):
                for q in (0, 1):
                    part = got[i, 4 : 4 + span, q * 128 : (q + 1) * 128]
                    up[i, 2 * c + q, pl.ds(0, span, 2), :] = part
                    up[i, 2 * c + q, pl.ds(1, span, 2), :] = part

        for p in range(count + 2 * depth):
            for c in range(cols // 64):
                lanes = pl.ds(c * 128, 128)
                vpad[p, :, lanes] = vpad[p, :, lanes] + up[(p + depth % 2) // 2, c]

    rows2 = pl.ds(pl.multiple_of(n * y2, 8), y2 + 16)
    prolong(v2[pl.ds(w * x2, x2 + 2), rows2, :], v1, up1, x1, y1, 2)
    half_sweep1(range(2, x1 + 2), True)
    start1(V1, v1)
    finish1(V1, v1)
    half_sweep1(range(1, x1 + 3), False)

    prolong(v1[1 : x1 + 3], v0, up0, x0, y0, 1)
    half_sweep(v0, w0, s0, *level0, True, part="edge")
    start_wide(V0C, 0, v0)
    half_sweep(v0, w0, s0, *level0, True, part="inner")
    start_narrow(V0C, 0, v0)
    finish_narrow(V0C, 0, v0)
    half_sweep(v0, w0, s0, *level0, False, out=out_ref, part="inner")
    results = [
        pltpu.make_async_copy(out_ref.at[planes], out_hbm.at[planes], ls.at[2 + m])
        for m, planes in enumerate((pl.ds(1, x0 - 2), pl.ds(0, 1), pl.ds(x0 - 1, 1)))
    ]
    results[0].start()
    finish_wide(V0C, 0, v0)
    half_sweep(v0, w0, s0, *level0, False, out=out_ref, part="edge")
    results[1].start()
    results[2].start()
    for copy in results:
        copy.wait()


def solution(mesh):
    wn, nn = mesh.shape["wide"], mesh.shape["narrow"]
    placed = P("wide", "narrow", None)

    def on_device(sources, permeability):
        x0, y0, z0 = sources.shape
        x1, y1, z1 = x0 // 2, y0 // 2, z0 // 2
        x2, y2, z2 = x1 // 2, y1 // 2, z1 // 2
        gx, gy = x2 * wn, y2 * nn
        px, y3 = gx // 4, gy // 2
        pad0, pad1, pad2 = (x0 + 2, y0 + 16, z0), (x1 + 4, y1 + 16, z1), (gx + 2, gy + 16, z2)
        l0, l1, l2 = (x0, y0, z0), (x1, y1, z1), (gx, gy, z2)
        v = lambda *shape: pltpu.VMEM(shape, F32)
        scratch = [
            v(*pad0), v(*pad0), v(6, *l0), v(*l0), v(*l0),
            v(*pad1), v(*pad1), v(6, *pad1), v(*pad1), v(*pad1), v(*pad1), v(*l1), v(*l1),
            v(*pad2), v(*pad2), v(6, *l2), v(*l2), v(*l2), v(*l2), v(x2, y2, z2), v(x2, y2, z2),
            v(wn, nn, x2, y2, z2), v(wn, nn, x2, y2, z2),
            v(6, px, y3, 128), v(px, y3, 128),
            v(2, z0 // 128, max(y0, gy), 128), v(x1, y1, z0), v(x2, y2, z1), v(px, y3, 256),
            v(x1 + 2, z0 // 128, y0 + 16, 128), v(x2 + 2, z1 // 128, y1 + 16, 128), v(gx // 2, gy, z2),
            v(256, 128), v(128, 256),
            v(4, 2, y0 // 2, z0), v(4, 2, y0 // 2, z0), v(4, 2, 8, z0), v(4, 2, 8, z0),
            v(2, 2, y1, z1), v(2, 2, y1, z1), v(3, 2, 2 * x1, z1), v(3, 2, 2 * x1, z1),
            v(3, 2, 2, 1, z1), v(3, 2, 2, 1, z1),
            pltpu.SemaphoreType.DMA((4, 4)), pltpu.SemaphoreType.DMA((4, 4)),
            pltpu.SemaphoreType.DMA((3, 8)), pltpu.SemaphoreType.DMA((3, 8)),
            pltpu.SemaphoreType.DMA((2, wn - 1)), pltpu.SemaphoreType.DMA((2, wn - 1)),
            pltpu.SemaphoreType.DMA((2, wn, nn - 1)), pltpu.SemaphoreType.DMA((2, wn, nn - 1)),
            v(*l0), v(*l0), pltpu.SemaphoreType.DMA((5,)),
        ]
        return pl.pallas_call(
            functools.partial(kernel, (wn, nn)),
            out_shape=jax.ShapeDtypeStruct(sources.shape, F32),
            in_specs=[pl.BlockSpec(memory_space=pltpu.HBM)] * 2,
            out_specs=pl.BlockSpec(memory_space=pltpu.HBM),
            scratch_shapes=scratch,
            compiler_params=pltpu.CompilerParams(
                collective_id=0, has_side_effects=True, vmem_limit_bytes=60 * 1024 * 1024
            ),
        )(sources, permeability)

    return jax.shard_map(
        on_device, mesh=mesh, in_specs=(placed, placed), out_specs=placed, check_vma=False
    )
```

```python
import functools

import jax
import jax.numpy as jnp
from jax import lax
from jax.experimental import pallas as pl
from jax.experimental.pallas import tpu as pltpu
from jax.sharding import PartitionSpec as P

CSWEEPS = 16
F32 = jnp.float32
MESH = pl.DeviceIdType.MESH
K0, V0A, V0B, V0C = range(4)
K1, S1, V1 = range(3)


def iota(shape, dim):
    return lax.broadcasted_iota(jnp.int32, shape, dim)


def red_cells(shape, plane):
    total = iota(shape, 0) + iota(shape, 1) + plane
    return (total & 1) == 0


def matmul(left, right):
    result = None
    for _ in range(3):
        part = left.astype(jnp.bfloat16)
        left = left - part.astype(F32)
        term = jnp.dot(part, right, preferred_element_type=F32)
        result = term if result is None else result + term
    return result


def each_plane(count, step, body, part="all"):
    if part == "edge":
        body(0)
        body(count - 1)
        return
    low, high = (1, count - 1) if part == "inner" else (0, count)
    if high - low == step:
        for i in range(low, high):
            body(i)
        return

    @pl.loop(0, (high - low) // step)
    def _(chunk):
        for i in range(step):
            body(low + chunk * step + i)


def shift(array, amount, axis):
    return pltpu.roll(array, amount % array.shape[axis], axis)


def coefficients(kpad, weights, diag, scaled, right, square, rows, count, step, part="all"):
    def body(i):
        k = kpad[i + 1, 8 : 8 + rows, :]
        lane = iota(k.shape, 1)
        last = k.shape[1] - 1
        up = jnp.where(lane == last, 0.0, shift(k, -1, 1))
        down = jnp.where(lane == 0, 0.0, shift(k, 1, 1))
        faces = [
            kpad[i + 2, 8 : 8 + rows, :],
            kpad[i, 8 : 8 + rows, :],
            kpad[i + 1, 9 : 9 + rows, :],
            kpad[i + 1, 7 : 7 + rows, :],
            up,
            down,
        ]
        faces = [0.5 * (k + face) for face in faces]
        total = functools.reduce(lambda a, b: a + b, faces)
        inverse = 1.0 / total
        for n, face in enumerate(faces):
            w = face * inverse
            if n == 4:
                w = jnp.where(lane == last, 0.0, w)
            if n == 5:
                w = jnp.where(lane == 0, 0.0, w)
            weights[n, i] = w
        diag[i] = total * (1.0 / square)
        if right is not None:
            scaled[i] = (square * inverse) * right[i]
        else:
            scaled[i] = square * inverse

    each_plane(count, step, body, part)


def updated(vpad, weights, scaled, i, rows):
    v = vpad[i + 1, 8 : 8 + rows, :]
    a = weights[0, i] * vpad[i + 2, 8 : 8 + rows, :] + weights[1, i] * vpad[i, 8 : 8 + rows, :]
    b = (
        weights[2, i] * vpad[i + 1, 9 : 9 + rows, :]
        + weights[3, i] * vpad[i + 1, 7 : 7 + rows, :]
    )
    c = weights[4, i] * shift(v, -1, 1) + weights[5, i] * shift(v, 1, 1)
    return v, (scaled[i] + a) + (b + c)


def first_red(vpad, scaled, rows, count, step, part="all"):
    def body(i):
        s = scaled[i]
        vpad[i + 1, 8 : 8 + rows, :] = jnp.where(red_cells(s.shape, i), s, 0.0)

    each_plane(count, step, body, part)


def half_sweep(vpad, weights, scaled, rows, count, step, red, out=None, part="all"):
    def body(i):
        v, new = updated(vpad, weights, scaled, i, rows)
        cells = red_cells(v.shape, i)
        value = jnp.where(cells, new, v) if red else jnp.where(cells, v, new)
        if out is None:
            vpad[i + 1, 8 : 8 + rows, :] = value
        else:
            out[i] = value

    each_plane(count, step, body, part)


def restrict_pair(first, second, tmp, slot):
    half = first.shape[0] // 2
    total = first + second
    parts = []
    for c in range(first.shape[1] // 128):
        tmp[slot, c, : 2 * half, :] = total[:, c * 128 : (c + 1) * 128]
        parts.append(tmp[slot, c, pl.ds(0, half, 2), :] + tmp[slot, c, pl.ds(1, half, 2), :])
    return parts


def kernel(sizes, b_hbm, k_hbm, out_hbm, *s):
    wn, nn = sizes
    (kp0, v0, w0, d0, s0, kp1, v1, w1, d1, s1, f1, b1, k1, kp2, v2, w2, d2, s2, f2, b2l, k2l,
     gk, gb, w3, s3, tmp, half0, half1, half2, up0, up1, up2, rmat, pmat,
     ws0, wr0, ns0, nr0, ws1, wr1, ns1, nr1, cs1, cr1,
     hs, hr, hs1, hr1, gsa, gra, gsb, grb, b_ref, out_ref, ls) = s
    x0, y0, z0 = b_hbm.shape
    half_y0 = y0 // 2
    x1, y1, z1 = x0 // 2, y0 // 2, z0 // 2
    x2, y2, z2 = x1 // 2, y1 // 2, z1 // 2
    gx, gy = x2 * wn, y2 * nn
    px = gx // 4
    y3 = gy // 2
    w, n = lax.axis_index("wide"), lax.axis_index("narrow")

    def wide(d):
        return (lax.rem(w + d, wn), n)

    def narrow(d):
        return (w, lax.rem(n + d, nn))

    def diagonal(a, c):
        return (lax.rem(w + (1 if a else wn - 1), wn), lax.rem(n + (1 if c else nn - 1), nn))

    corners = [(a, c) for a in (0, 1) for c in (0, 1)]
    barrier = pltpu.get_barrier_semaphore()
    for a, c in corners:
        pl.semaphore_signal(barrier, inc=1, device_id=diagonal(a, c), device_id_type=MESH)
    for d in range(1, wn):
        pl.semaphore_signal(barrier, inc=1, device_id=wide(d), device_id_type=MESH)
    for d in range(1, nn):
        pl.semaphore_signal(barrier, inc=1, device_id=narrow(d), device_id_type=MESH)

    inside = pl.ds(8, y0)
    k_in = pltpu.make_async_copy(k_hbm, kp0.at[pl.ds(1, x0), inside, :], ls.at[0])
    k_in.start()
    b_in = pltpu.make_async_copy(b_hbm, b_ref, ls.at[1])
    b_in.start()

    @pl.when(w == 0)
    def _():
        kp0[0] = jnp.zeros(kp0.shape[1:], F32)

    @pl.when(w == wn - 1)
    def _():
        kp0[x0 + 1] = jnp.zeros(kp0.shape[1:], F32)

    rmat[...] = jnp.where(iota((256, 128), 0) // 2 == iota((256, 128), 1), 1.0, 0.0).astype(jnp.bfloat16)
    pmat[...] = jnp.where(iota((128, 256), 0) == iota((128, 256), 1) // 2, 1.0, 0.0).astype(jnp.bfloat16)

    def clear(pad, rows, ends=True):
        planes = pad.shape[0]
        zero = jnp.zeros(pad.shape[1:], F32)
        strip = jnp.zeros((8, pad.shape[2]), F32)
        if ends:
            pad[0] = zero
            pad[planes - 1] = zero

        @pl.loop(1, planes - 1)
        def _(i):
            pad[i, 0:8, :] = strip
            pad[i, 8 + rows : 16 + rows, :] = strip

    def buffers(rnd, level):
        return (ws0, wr0, ns0, nr0, rnd, x0, y0)

    def wide_copies(rnd, level):
        ws, wr, _, _, r, _, _ = buffers(rnd, level)
        specs = []
        for side in (0, 1):
            if rnd == K0:
                src = k_hbm.at[(0, x0 - 1)[side]]
                dst = kp0.at[(x0 + 1, 0)[side], inside, :]
            else:
                src, dst = ws.at[r, side], wr.at[r, 1 - side]
            specs.append((
                w > 0 if side == 0 else w < wn - 1,
                w < wn - 1 if side == 0 else w > 0,
                pltpu.make_async_remote_copy(
                    src_ref=src, dst_ref=dst,
                    send_sem=hs.at[rnd, side], recv_sem=hr.at[rnd, side],
                    device_id=wide(wn - 1 if side == 0 else 1), device_id_type=MESH),
            ))
        return specs

    def narrow_copies(rnd, level):
        _, _, ns, nr, r, _, _ = buffers(rnd, level)
        specs = []
        for side in (0, 1):
            specs.append((
                n > 0 if side == 0 else n < nn - 1,
                n < nn - 1 if side == 0 else n > 0,
                pltpu.make_async_remote_copy(
                    src_ref=ns.at[r, side], dst_ref=nr.at[r, 1 - side],
                    send_sem=hs.at[rnd, 2 + side], recv_sem=hr.at[rnd, 2 + side],
                    device_id=narrow(nn - 1 if side == 0 else 1), device_id_type=MESH),
            ))
        return specs

    def start_all(specs):
        for sends, _, copy in specs:
            @pl.when(sends)
            def _(copy=copy):
                copy.start()

    def finish_all(specs):
        for sends, receives, copy in specs:
            @pl.when(receives)
            def _(copy=copy):
                copy.wait_recv()

            @pl.when(sends)
            def _(copy=copy):
                copy.wait_send()

    def colour_of(rnd, plane):
        cells = red_cells((half_y0, z0), plane)
        return jnp.logical_not(cells) if rnd == V0B else cells

    def start_wide(rnd, level, pad):
        ws, _, _, _, r, count, rows = buffers(rnd, level)
        if rnd != K0:
            for side, i in ((0, 0), (1, count - 1)):
                face = pad[i + 1, 8 : 8 + rows, :]
                if level == 0:
                    cells = colour_of(rnd, i)
                    face = jnp.where(cells, face[:half_y0], shift(face[half_y0:], 1, 1))
                ws[r, side] = face
        start_all(wide_copies(rnd, level))

    def start_narrow(rnd, level, pad):
        _, _, ns, _, r, count, rows = buffers(rnd, level)
        for i in range(count):
            ns[r, 0, i : i + 1, :] = pad[i + 1, 8:9, :]
            ns[r, 1, i : i + 1, :] = pad[i + 1, 7 + rows : 8 + rows, :]
        start_all(narrow_copies(rnd, level))

    def finish_wide(rnd, level, pad):
        _, wr, _, _, r, count, rows = buffers(rnd, level)
        finish_all(wide_copies(rnd, level))
        if rnd == K0:
            return
        for side, i in ((0, -1), (1, count)):
            @pl.when(w > 0 if side == 0 else w < wn - 1)
            def _(side=side, i=i):
                got = wr[r, side]
                if level == 0:
                    cells = colour_of(rnd, i)
                    upper, lower = pl.ds(8, half_y0), pl.ds(8 + half_y0, half_y0)
                    pad[i + 1, upper, :] = jnp.where(cells, got, pad[i + 1, upper, :])
                    pad[i + 1, lower, :] = jnp.where(
                        cells, shift(got, -1, 1), pad[i + 1, lower, :]
                    )
                else:
                    pad[i + 1, 8 : 8 + rows, :] = got

    def finish_narrow(rnd, level, pad):
        _, _, _, nr, r, count, rows = buffers(rnd, level)
        finish_all(narrow_copies(rnd, level))

        @pl.when(n > 0)
        def _():
            for i in range(count):
                pad[i + 1, 7:8, :] = nr[r, 0, i : i + 1, :]

        @pl.when(n < nn - 1)
        def _():
            for i in range(count):
                pad[i + 1, 8 + rows : 9 + rows, :] = nr[r, 1, i : i + 1, :]

    def halo_start(rnd, level, pad):
        start_wide(rnd, level, pad)
        start_narrow(rnd, level, pad)

    def halo_finish(rnd, level, pad):
        finish_narrow(rnd, level, pad)
        finish_wide(rnd, level, pad)

    pl.semaphore_wait(barrier, wn - 1 + nn - 1 + len(corners))
    start_wide(K0, 0, kp0)
    k_in.wait()
    start_narrow(K0, 0, kp0)

    own1 = pl.ds(8, y1)

    def exists(a, c):
        good = None
        for side, at, size in ((a, w, wn), (c, n, nn)):
            if side is not None:
                here = at < size - 1 if side else at > 0
                good = here if good is None else jnp.logical_and(good, here)
        return good

    def copies1(rnd, array):
        specs = []

        def add(slot, a, c, src, dst, target):
            back = [None if side is None else 1 - side for side in (a, c)]
            specs.append((exists(a, c), exists(*back), pltpu.make_async_remote_copy(
                src_ref=src, dst_ref=dst, send_sem=hs1.at[rnd, slot],
                recv_sem=hr1.at[rnd, slot], device_id=target, device_id_type=MESH)))

        for a, c in corners:
            add(4 + 2 * a + c, a, c, cs1.at[rnd, a, c], cr1.at[rnd, 1 - a, 1 - c],
                diagonal(a, c))
        for side in (0, 1):
            if rnd == V1:
                src, dst = ws1.at[side], wr1.at[1 - side]
            else:
                src = array.at[pl.ds((2, x1)[side], 2), own1, :]
                dst = array.at[pl.ds((x1 + 2, 0)[side], 2), own1, :]
            add(side, side, None, src, dst, wide(1 if side else wn - 1))
        for side in (0, 1):
            add(2 + side, None, side, ns1.at[rnd, side], nr1.at[rnd, 1 - side],
                narrow(1 if side else nn - 1))
        return specs

    def start1(rnd, array):
        for a, c in corners:
            row = (8, 7 + y1)[c]
            cs1[rnd, a, c] = array[(2, x1 + 1)[a], row : row + 1, :]
        if rnd == V1:
            ws1[0] = array[2:4, 8 : 8 + y1, :]
            ws1[1] = array[x1 : x1 + 2, 8 : 8 + y1, :]
        for i in range(x1):
            ns1[rnd, 0, 2 * i : 2 * i + 2, :] = array[2 + i, 8:10, :]
            ns1[rnd, 1, 2 * i : 2 * i + 2, :] = array[2 + i, 6 + y1 : 8 + y1, :]
        start_all(copies1(rnd, array))

    def finish1(rnd, array):
        finish_all(copies1(rnd, array)[::-1])
        for side in (0, 1):
            if rnd == V1:
                @pl.when(exists(side, None))
                def _(side=side):
                    at = (0, x1 + 2)[side]
                    array[at : at + 2, 8 : 8 + y1, :] = wr1[side]

            @pl.when(exists(None, side))
            def _(side=side):
                at = (6, 8 + y1)[side]
                for i in range(x1):
                    array[2 + i, at : at + 2, :] = nr1[rnd, side, 2 * i : 2 * i + 2, :]

        for a, c in corners:
            @pl.when(exists(a, c))
            def _(a=a, c=c):
                at = (7, 8 + y1)[c]
                array[(1, x1 + 2)[a], at : at + 1, :] = cr1[rnd, a, c]

    def clear1(array):
        strip = jnp.zeros((8, z1), F32)
        for p in range(x1 + 4):
            array[p, 0:8, :] = strip
            array[p, 8 + y1 :, :] = strip

        for side in (0, 1):
            @pl.when(jnp.logical_not(exists(side, None)))
            def _(side=side):
                at = (0, x1 + 2)[side]
                array[at : at + 2, 8 : 8 + y1, :] = jnp.zeros((2, y1, z1), F32)

    def coefficients1():
        for j in range(1, x1 + 3):
            k = kp1[j]
            lane = iota(k.shape, 1)
            first, last = lane == 0, lane == z1 - 1
            faces = [kp1[j + 1], kp1[j - 1], shift(k, -1, 0), shift(k, 1, 0),
                     jnp.where(last, 0.0, shift(k, -1, 1)), jnp.where(first, 0.0, shift(k, 1, 1))]
            faces = [0.5 * (k + face) for face in faces]
            total = functools.reduce(lambda a, b: a + b, faces)
            inverse = jnp.where(k > 0.0, 1.0 / total, 0.0)
            for m, face in enumerate(faces):
                weight = face * inverse
                if m >= 4:
                    weight = jnp.where(first if m == 5 else last, 0.0, weight)
                w1[m, j] = weight
            d1[j] = total * 0.25
            f1[j] = 4.0 * inverse

    def updated1(j):
        v = v1[j]
        a = w1[0, j] * v1[j + 1] + w1[1, j] * v1[j - 1]
        b = w1[2, j] * shift(v, -1, 0) + w1[3, j] * shift(v, 1, 0)
        c = w1[4, j] * shift(v, -1, 1) + w1[5, j] * shift(v, 1, 1)
        return v, (s1[j] + a) + (b + c)

    def half_sweep1(planes, red):
        for j in planes:
            v, new = updated1(j)
            cells = red_cells(v.shape, j)
            v1[j] = jnp.where(cells, new, v) if red else jnp.where(cells, v, new)

    def gather_wide(g, which, local):
        copies = []
        for d in range(1, wn):
            copies.append(pltpu.make_async_remote_copy(
                src_ref=local, dst_ref=g.at[w, n],
                send_sem=gsa.at[which, d - 1], recv_sem=gra.at[which, d - 1],
                device_id=wide(d), device_id_type=MESH))
        return copies

    near_first = sorted(range(1, wn), key=lambda d: min(d, wn - d))

    def relay_copies(g, which, d, local):
        at = lax.rem(w + wn - d, wn)
        return [
            pltpu.make_async_remote_copy(
                src_ref=local if d == 0 else g.at[at, n], dst_ref=g.at[at, n],
                send_sem=gsb.at[which, d, e - 1], recv_sem=grb.at[which, d, e - 1],
                device_id=narrow(e), device_id_type=MESH)
            for e in range(1, nn)
        ]

    def gather_start(g, which, local):
        for copy in gather_wide(g, which, local)[::-1]:
            copy.start()
        for copy in relay_copies(g, which, 0, local):
            copy.start()

    def gather_relay(g, which, local):
        arriving = gather_wide(g, which, local)
        for d in near_first:
            arriving[d - 1].wait_recv()
            for copy in relay_copies(g, which, d, local):
                copy.start()

    def gather_finish(g, which, local):
        for d in [0] + near_first:
            for copy in relay_copies(g, which, d, local):
                copy.wait_recv()
        for d in [0] + near_first:
            for copy in relay_copies(g, which, d, local):
                copy.wait_send()
        for copy in gather_wide(g, which, local):
            copy.wait_send()

    for i in range(x1):
        for c, part in enumerate(restrict_pair(kp0[2 * i + 1, inside, :], kp0[2 * i + 2, inside, :], tmp, i % 2)):
            half0[i, :, pl.ds(c * 128, 128)] = part

    def lanes_down(half, store, planes, rows, cols):
        flat = half[...].reshape(planes * rows, cols)
        for c in range(cols // 256):
            got = matmul(flat[:, c * 256 : (c + 1) * 256], rmat[...]) * 0.125
            store(c, got.reshape(planes, rows, 128))

    def store_k1(c, got):
        k1[:, :, pl.ds(c * 128, 128)] = got
        kp1[2 : 2 + x1, 8 : 8 + y1, pl.ds(c * 128, 128)] = got

    lanes_down(half0, store_k1, x1, y1, z0)
    clear1(kp1)
    clear1(s1)
    start1(K1, kp1)
    for i in range(x2):
        for c, part in enumerate(restrict_pair(k1[2 * i], k1[2 * i + 1], tmp, i % 2)):
            half1[i, :, pl.ds(c * 128, 128)] = part

    def store_k2(c, got):
        k2l[...] = got
        gk[w, n] = got

    lanes_down(half1, store_k2, x2, y2, z1)
    gather_start(gk, 0, k2l)
    clear(kp0, y0, ends=False)
    for pad, rows in ((v0, y0), (kp2, gy), (v2, gy)):
        clear(pad, rows)

    b_in.wait()
    finish_narrow(K0, 0, kp0)
    finish_wide(K0, 0, kp0)
    level0 = (y0, x0, 2)
    for part in ("edge", "inner"):
        coefficients(kp0, w0, d0, s0, b_ref, 1.0, *level0, part=part)
        first_red(v0, s0, *level0, part=part)
        if part == "edge":
            start_wide(V0A, 0, v0)
    start_narrow(V0A, 0, v0)
    finish1(K1, kp1)
    coefficients1()
    halo_finish(V0A, 0, v0)
    half_sweep(v0, w0, s0, *level0, False, part="edge")
    start_wide(V0B, 0, v0)
    half_sweep(v0, w0, s0, *level0, False, part="inner")
    start_narrow(V0B, 0, v0)
    gather_relay(gk, 0, k2l)
    finish_narrow(V0B, 0, v0)

    def residual(vpad, weights, scaled, diag, i, rows):
        v, new = updated(vpad, weights, scaled, i, rows)
        return diag[i] * (new - v)

    def restrict0(i, slot):
        first = residual(v0, w0, s0, d0, 2 * i, y0)
        second = residual(v0, w0, s0, d0, 2 * i + 1, y0)
        for c, part in enumerate(restrict_pair(first, second, tmp, slot)):
            half0[i, :, pl.ds(c * 128, 128)] = part

    @pl.loop(1, x1 - 1)
    def _(i):
        restrict0(i, 0)

    finish_wide(V0B, 0, v0)
    restrict0(0, 0)
    restrict0(x1 - 1, 1)

    def store_b1(c, got):
        b1[:, :, pl.ds(c * 128, 128)] = got

    lanes_down(half0, store_b1, x1, y1, z0)

    for i in range(x1):
        s1[2 + i, own1, :] = f1[2 + i, own1, :] * b1[i]
    start1(S1, s1)
    gather_finish(gk, 0, k2l)
    for a in range(wn):
        for c in range(nn):
            kp2[1 + a * x2 : 1 + (a + 1) * x2, 8 + c * y2 : 8 + (c + 1) * y2, :] = gk[a, c]
    coefficients(kp2, w2, d2, f2, None, 16.0, gy, gx, 8)

    def pack_down(get, tag):
        @pl.loop(0, px)
        def _(i):
            for h in (0, 1):
                part = restrict_pair(*get(i + h * px), tmp, h)[0]
                half2[i, :, pl.ds(h * 128, 128)] = part

        return matmul(half2[...].reshape(px * y3, 256), rmat[...]).reshape(px, y3, 128) * 0.125

    def plane_of(i):
        return kp2[1 + 2 * i, 8 : 8 + gy, :], kp2[2 + 2 * i, 8 : 8 + gy, :]

    k3 = pack_down(plane_of, 0)
    shape3 = (px, y3, 128)
    p_at, r_at, l_at = iota(shape3, 0), iota(shape3, 1), iota(shape3, 2)
    z_at = l_at & 63
    outside = [
        (p_at == px - 1) & (l_at >= 64),
        (p_at == 0) & (l_at < 64),
        r_at == y3 - 1,
        r_at == 0,
        z_at == 63,
        z_at == 0,
    ]

    def neighbours(v):
        xp = jnp.concatenate([v[1:], shift(v[:1], 64, 2)], axis=0)
        xm = jnp.concatenate([shift(v[-1:], 64, 2), v[:-1]], axis=0)
        return [xp, xm, shift(v, -1, 1), shift(v, 1, 1), shift(v, -1, 2), shift(v, 1, 2)]

    faces3 = [
        0.5 * (k3 + jnp.where(out, 0.0, near)) for out, near in zip(outside, neighbours(k3))
    ]
    total3 = functools.reduce(lambda a, b: a + b, faces3)
    inverse3 = 1.0 / total3
    for m in range(6):
        w3[m] = jnp.where(outside[m], 0.0, faces3[m] * inverse3)
    s3[...] = 64.0 * inverse3

    finish1(S1, s1)
    for j in range(x1 + 4):
        v1[j] = jnp.where(red_cells((y1 + 16, z1), j), s1[j], 0.0)
    half_sweep1(range(1, x1 + 3), False)

    def residual1(i):
        v, new = updated1(2 + i)
        return (d1[2 + i] * (new - v))[8 : 8 + y1]

    for i in range(x2):
        first, second = residual1(2 * i), residual1(2 * i + 1)
        for c, part in enumerate(restrict_pair(first, second, tmp, i % 2)):
            half1[i, :, pl.ds(c * 128, 128)] = part

    def store_b2(c, got):
        b2l[...] = got
        gb[w, n] = got

    lanes_down(half1, store_b2, x2, y2, z1)
    gather_start(gb, 1, b2l)

    gather_relay(gb, 1, b2l)
    gather_finish(gb, 1, b2l)

    for a in range(wn):
        for c in range(nn):
            for i in range(x2):
                rows = pl.ds(c * y2, y2)
                s2[a * x2 + i, rows, :] = f2[a * x2 + i, rows, :] * gb[a, c, i]
    first_red(v2, s2, gy, gx, 8)
    half_sweep(v2, w2, s2, gy, gx, 8, False)

    def resid2(i):
        return (residual(v2, w2, s2, d2, 2 * i, gy), residual(v2, w2, s2, d2, 2 * i + 1, gy))

    b3 = pack_down(resid2, 1)
    scaled3 = s3[...] * b3
    s3[...] = scaled3
    first_at = p_at + jnp.where(l_at >= 64, px, 0)
    red3 = ((first_at + r_at + z_at) & 1) == 0

    def sweep3(e, red):
        near = neighbours(e)
        terms = [w3[m] * near[m] for m in range(6)]
        new = ((s3[...] + terms[0]) + (terms[1] + terms[2])) + ((terms[3] + terms[4]) + terms[5])
        return jnp.where(red3, new, e) if red else jnp.where(red3, e, new)

    e = jnp.where(red3, scaled3, 0.0)
    e = sweep3(e, False)

    def sweeps3(_, e):
        for _ in range(5):
            e = sweep3(sweep3(e, True), False)
        return e

    e = lax.fori_loop(0, (CSWEEPS - 1) // 5, sweeps3, e)
    for _ in range((CSWEEPS - 1) % 5):
        e = sweep3(sweep3(e, True), False)

    wide3 = matmul(e.reshape(px * y3, 128), pmat[...]).reshape(px, y3, 256)
    for h in (0, 1):
        part = wide3[:, :, h * 128 : (h + 1) * 128]
        for i in range(px):
            up2[h * px + i, pl.ds(0, y3, 2), :] = part[i]
            up2[h * px + i, pl.ds(1, y3, 2), :] = part[i]

    def planes_from(first, count, limit):
        return jnp.clip(first, 0, limit - count)

    begin = planes_from(w * x2 // 2 - 2, x2 // 2 + 4, gx // 2)
    for m in range(x2 // 2 + 4):
        i = begin + m
        add = up2[i]
        for j in (1, 2):
            v2[2 * i + j, 8 : 8 + gy, :] = v2[2 * i + j, 8 : 8 + gy, :] + add

    for depth, red in ((2, True), (1, False)):
        count = x2 + 2 * depth
        begin = planes_from(w * x2 - depth, count, gx)
        for m in range(count):
            i = begin + m
            v, new = updated(v2, w2, s2, i, gy)
            cells = red_cells(v.shape, i)
            v2[i + 1, 8 : 8 + gy, :] = jnp.where(cells, new, v) if red else jnp.where(cells, v, new)

    def prolong(coarse, vpad, up, count, rows, depth):
        planes, crows, cols = coarse.shape
        flat = coarse.reshape(planes * crows, cols)
        span = (rows + 16) // 2
        for c in range(cols // 128):
            got = matmul(flat[:, c * 128 : (c + 1) * 128], pmat[...])
            got = got.reshape(planes, crows, 256)
            for i in range(planes):
                for q in (0, 1):
                    part = got[i, 4 : 4 + span, q * 128 : (q + 1) * 128]
                    up[i, 2 * c + q, pl.ds(0, span, 2), :] = part
                    up[i, 2 * c + q, pl.ds(1, span, 2), :] = part

        for p in range(count + 2 * depth):
            for c in range(cols // 64):
                lanes = pl.ds(c * 128, 128)
                vpad[p, :, lanes] = vpad[p, :, lanes] + up[(p + depth % 2) // 2, c]

    rows2 = pl.ds(pl.multiple_of(n * y2, 8), y2 + 16)
    prolong(v2[pl.ds(w * x2, x2 + 2), rows2, :], v1, up1, x1, y1, 2)
    half_sweep1(range(2, x1 + 2), True)
    start1(V1, v1)
    finish1(V1, v1)
    half_sweep1(range(1, x1 + 3), False)

    prolong(v1[1 : x1 + 3], v0, up0, x0, y0, 1)
    half_sweep(v0, w0, s0, *level0, True, part="edge")
    start_wide(V0C, 0, v0)
    half_sweep(v0, w0, s0, *level0, True, part="inner")
    start_narrow(V0C, 0, v0)
    finish_narrow(V0C, 0, v0)
    half_sweep(v0, w0, s0, *level0, False, out=out_ref, part="inner")
    results = [
        pltpu.make_async_copy(out_ref.at[planes], out_hbm.at[planes], ls.at[2 + m])
        for m, planes in enumerate((pl.ds(1, x0 - 2), pl.ds(0, 1), pl.ds(x0 - 1, 1)))
    ]
    results[0].start()
    finish_wide(V0C, 0, v0)
    half_sweep(v0, w0, s0, *level0, False, out=out_ref, part="edge")
    results[1].start()
    results[2].start()
    for copy in results:
        copy.wait()


def solution(mesh):
    wn, nn = mesh.shape["wide"], mesh.shape["narrow"]
    placed = P("wide", "narrow", None)

    def on_device(sources, permeability):
        x0, y0, z0 = sources.shape
        x1, y1, z1 = x0 // 2, y0 // 2, z0 // 2
        x2, y2, z2 = x1 // 2, y1 // 2, z1 // 2
        gx, gy = x2 * wn, y2 * nn
        px, y3 = gx // 4, gy // 2
        pad0, pad1, pad2 = (x0 + 2, y0 + 16, z0), (x1 + 4, y1 + 16, z1), (gx + 2, gy + 16, z2)
        l0, l1, l2 = (x0, y0, z0), (x1, y1, z1), (gx, gy, z2)
        v = lambda *shape: pltpu.VMEM(shape, F32)
        scratch = [
            v(*pad0), v(*pad0), v(6, *l0), v(*l0), v(*l0),
            v(*pad1), v(*pad1), v(6, *pad1), v(*pad1), v(*pad1), v(*pad1), v(*l1), v(*l1),
            v(*pad2), v(*pad2), v(6, *l2), v(*l2), v(*l2), v(*l2), v(x2, y2, z2), v(x2, y2, z2),
            v(wn, nn, x2, y2, z2), v(wn, nn, x2, y2, z2),
            v(6, px, y3, 128), v(px, y3, 128),
            v(2, z0 // 128, max(y0, gy), 128), v(x1, y1, z0), v(x2, y2, z1), v(px, y3, 256),
            v(x1 + 2, z0 // 128, y0 + 16, 128), v(x2 + 2, z1 // 128, y1 + 16, 128), v(gx // 2, gy, z2),
            pltpu.VMEM((256, 128), jnp.bfloat16), pltpu.VMEM((128, 256), jnp.bfloat16),
            v(4, 2, y0 // 2, z0), v(4, 2, y0 // 2, z0), v(4, 2, 8, z0), v(4, 2, 8, z0),
            v(2, 2, y1, z1), v(2, 2, y1, z1), v(3, 2, 2 * x1, z1), v(3, 2, 2 * x1, z1),
            v(3, 2, 2, 1, z1), v(3, 2, 2, 1, z1),
            pltpu.SemaphoreType.DMA((4, 4)), pltpu.SemaphoreType.DMA((4, 4)),
            pltpu.SemaphoreType.DMA((3, 8)), pltpu.SemaphoreType.DMA((3, 8)),
            pltpu.SemaphoreType.DMA((2, wn - 1)), pltpu.SemaphoreType.DMA((2, wn - 1)),
            pltpu.SemaphoreType.DMA((2, wn, nn - 1)), pltpu.SemaphoreType.DMA((2, wn, nn - 1)),
            v(*l0), v(*l0), pltpu.SemaphoreType.DMA((5,)),
        ]
        return pl.pallas_call(
            functools.partial(kernel, (wn, nn)),
            out_shape=jax.ShapeDtypeStruct(sources.shape, F32),
            in_specs=[pl.BlockSpec(memory_space=pltpu.HBM)] * 2,
            out_specs=pl.BlockSpec(memory_space=pltpu.HBM),
            scratch_shapes=scratch,
            compiler_params=pltpu.CompilerParams(
                collective_id=0, has_side_effects=True, vmem_limit_bytes=60 * 1024 * 1024
            ),
        )(sources, permeability)

    return jax.shard_map(
        on_device, mesh=mesh, in_specs=(placed, placed), out_specs=placed, check_vma=False
    )
```

```python
import functools

import jax
import jax.numpy as jnp
from jax import lax
from jax.experimental import pallas as pl
from jax.experimental.pallas import tpu as pltpu
from jax.sharding import PartitionSpec as P

CSWEEPS = 16
F32 = jnp.float32
MESH = pl.DeviceIdType.MESH
K0, V0A, V0B, V0C = range(4)
K1, S1, V1 = range(3)


def iota(shape, dim):
    return lax.broadcasted_iota(jnp.int32, shape, dim)


def red_cells(shape, plane):
    total = iota(shape, 0) + iota(shape, 1) + plane
    return (total & 1) == 0


def matmul(left, right):
    result = None
    for _ in range(3):
        part = left.astype(jnp.bfloat16)
        left = left - part.astype(F32)
        term = jnp.dot(part, right, preferred_element_type=F32)
        result = term if result is None else result + term
    return result


def each_plane(count, step, body, part="all"):
    if part == "edge":
        body(0)
        body(count - 1)
        return
    low, high = (1, count - 1) if part == "inner" else (0, count)
    if high - low == step:
        for i in range(low, high):
            body(i)
        return

    @pl.loop(0, (high - low) // step)
    def _(chunk):
        for i in range(step):
            body(low + chunk * step + i)


def shift(array, amount, axis):
    return pltpu.roll(array, amount % array.shape[axis], axis)


def coefficients(kpad, weights, diag, scaled, right, square, rows, count, step, part="all"):
    def body(i):
        k = kpad[i + 1, 8 : 8 + rows, :]
        lane = iota(k.shape, 1)
        last = k.shape[1] - 1
        up = jnp.where(lane == last, 0.0, shift(k, -1, 1))
        down = jnp.where(lane == 0, 0.0, shift(k, 1, 1))
        faces = [
            kpad[i + 2, 8 : 8 + rows, :],
            kpad[i, 8 : 8 + rows, :],
            kpad[i + 1, 9 : 9 + rows, :],
            kpad[i + 1, 7 : 7 + rows, :],
            up,
            down,
        ]
        faces = [0.5 * (k + face) for face in faces]
        total = functools.reduce(lambda a, b: a + b, faces)
        inverse = 1.0 / total
        for n, face in enumerate(faces):
            w = face * inverse
            if n == 4:
                w = jnp.where(lane == last, 0.0, w)
            if n == 5:
                w = jnp.where(lane == 0, 0.0, w)
            weights[n, i] = w
        diag[i] = total * (1.0 / square)
        if right is not None:
            scaled[i] = (square * inverse) * right[i]
        else:
            scaled[i] = square * inverse

    each_plane(count, step, body, part)


def updated(vpad, weights, scaled, i, rows):
    v = vpad[i + 1, 8 : 8 + rows, :]
    a = weights[0, i] * vpad[i + 2, 8 : 8 + rows, :] + weights[1, i] * vpad[i, 8 : 8 + rows, :]
    b = (
        weights[2, i] * vpad[i + 1, 9 : 9 + rows, :]
        + weights[3, i] * vpad[i + 1, 7 : 7 + rows, :]
    )
    c = weights[4, i] * shift(v, -1, 1) + weights[5, i] * shift(v, 1, 1)
    return v, (scaled[i] + a) + (b + c)


def first_red(vpad, scaled, rows, count, step, part="all"):
    def body(i):
        s = scaled[i]
        vpad[i + 1, 8 : 8 + rows, :] = jnp.where(red_cells(s.shape, i), s, 0.0)

    each_plane(count, step, body, part)


def half_sweep(vpad, weights, scaled, rows, count, step, red, out=None, part="all"):
    def body(i):
        v, new = updated(vpad, weights, scaled, i, rows)
        cells = red_cells(v.shape, i)
        value = jnp.where(cells, new, v) if red else jnp.where(cells, v, new)
        if out is None:
            vpad[i + 1, 8 : 8 + rows, :] = value
        else:
            out[i] = value

    each_plane(count, step, body, part)


def restrict_pair(first, second, tmp, slot):
    half = first.shape[0] // 2
    total = first + second
    parts = []
    for c in range(first.shape[1] // 128):
        tmp[slot, c, : 2 * half, :] = total[:, c * 128 : (c + 1) * 128]
        parts.append(tmp[slot, c, pl.ds(0, half, 2), :] + tmp[slot, c, pl.ds(1, half, 2), :])
    return parts


def kernel(sizes, b_hbm, k_hbm, out_hbm, *s):
    wn, nn = sizes
    (kp0, v0, w0, d0, s0, kp1, v1, w1, d1, s1, f1, b1, k1, kp2, v2, w2, d2, s2, f2, b2l, k2l,
     gk, gb, w3, s3, tmp, half0, half1, half2, up0, up1, up2, rmat, pmat,
     ws0, wr0, ns0, nr0, ws1, wr1, ns1, nr1, cs1, cr1,
     hs, hr, hs1, hr1, gsa, gra, gsb, grb, b_ref, out_ref, ls, meet) = s
    x0, y0, z0 = b_hbm.shape
    half_y0 = y0 // 2
    x1, y1, z1 = x0 // 2, y0 // 2, z0 // 2
    x2, y2, z2 = x1 // 2, y1 // 2, z1 // 2
    gx, gy = x2 * wn, y2 * nn
    px = gx // 4
    y3 = gy // 2
    w, n = lax.axis_index("wide"), lax.axis_index("narrow")

    def wide(d):
        return (lax.rem(w + d, wn), n)

    def narrow(d):
        return (w, lax.rem(n + d, nn))

    def diagonal(a, c):
        return (lax.rem(w + (1 if a else wn - 1), wn), lax.rem(n + (1 if c else nn - 1), nn))

    corners = [(a, c) for a in (0, 1) for c in (0, 1)]
    barrier = pltpu.get_barrier_semaphore()
    def count_of(*conditions):
        return sum(jnp.where(condition, 1, 0) for condition in conditions)

    def greet(sem, good, target):
        @pl.when(good)
        def _():
            pl.semaphore_signal(sem, inc=1, device_id=target, device_id_type=MESH)

    def on_wide(apart):
        return (
            (w >= apart, (lax.rem(w + wn - apart, wn), n)),
            (w + apart < wn, (lax.rem(w + apart, wn), n)),
        )

    for good, target in on_wide(1):
        greet(barrier, good, target)
    for d in range(1, nn):
        pl.semaphore_signal(barrier, inc=1, device_id=narrow(d), device_id_type=MESH)
    wide_good = (w > 0, w < wn - 1)
    narrow_good = (n > 0, n < nn - 1)
    for a, c in corners:
        greet(barrier, jnp.logical_and(wide_good[a], narrow_good[c]), diagonal(a, c))
    near = count_of(*wide_good) * (1 + count_of(*narrow_good)) + nn - 1

    meet_steps = [m for m in (1 << p for p in range(16)) if m < wn - 1]

    def meet_signal(p):
        for good, target in on_wide(meet_steps[p]):
            greet(meet.at[p], good, target)

    def meet_wait(p):
        pl.semaphore_wait(meet.at[p], count_of(*(good for good, _ in on_wide(meet_steps[p]))))

    inside = pl.ds(8, y0)
    k_in = pltpu.make_async_copy(k_hbm, kp0.at[pl.ds(1, x0), inside, :], ls.at[0])
    k_in.start()
    b_in = pltpu.make_async_copy(b_hbm, b_ref, ls.at[1])
    b_in.start()

    @pl.when(w == 0)
    def _():
        kp0[0] = jnp.zeros(kp0.shape[1:], F32)

    @pl.when(w == wn - 1)
    def _():
        kp0[x0 + 1] = jnp.zeros(kp0.shape[1:], F32)

    rmat[...] = jnp.where(iota((256, 128), 0) // 2 == iota((256, 128), 1), 1.0, 0.0).astype(jnp.bfloat16)
    pmat[...] = jnp.where(iota((128, 256), 0) == iota((128, 256), 1) // 2, 1.0, 0.0).astype(jnp.bfloat16)

    def clear(pad, rows, ends=True):
        planes = pad.shape[0]
        zero = jnp.zeros(pad.shape[1:], F32)
        strip = jnp.zeros((8, pad.shape[2]), F32)
        if ends:
            pad[0] = zero
            pad[planes - 1] = zero

        @pl.loop(1, planes - 1)
        def _(i):
            pad[i, 0:8, :] = strip
            pad[i, 8 + rows : 16 + rows, :] = strip

    def buffers(rnd, level):
        return (ws0, wr0, ns0, nr0, rnd, x0, y0)

    def wide_copies(rnd, level):
        ws, wr, _, _, r, _, _ = buffers(rnd, level)
        specs = []
        for side in (0, 1):
            if rnd == K0:
                src = k_hbm.at[(0, x0 - 1)[side]]
                dst = kp0.at[(x0 + 1, 0)[side], inside, :]
            else:
                src, dst = ws.at[r, side], wr.at[r, 1 - side]
            specs.append((
                w > 0 if side == 0 else w < wn - 1,
                w < wn - 1 if side == 0 else w > 0,
                pltpu.make_async_remote_copy(
                    src_ref=src, dst_ref=dst,
                    send_sem=hs.at[rnd, side], recv_sem=hr.at[rnd, side],
                    device_id=wide(wn - 1 if side == 0 else 1), device_id_type=MESH),
            ))
        return specs

    def narrow_copies(rnd, level):
        _, _, ns, nr, r, _, _ = buffers(rnd, level)
        specs = []
        for side in (0, 1):
            specs.append((
                n > 0 if side == 0 else n < nn - 1,
                n < nn - 1 if side == 0 else n > 0,
                pltpu.make_async_remote_copy(
                    src_ref=ns.at[r, side], dst_ref=nr.at[r, 1 - side],
                    send_sem=hs.at[rnd, 2 + side], recv_sem=hr.at[rnd, 2 + side],
                    device_id=narrow(nn - 1 if side == 0 else 1), device_id_type=MESH),
            ))
        return specs

    def start_all(specs):
        for sends, _, copy in specs:
            @pl.when(sends)
            def _(copy=copy):
                copy.start()

    def finish_all(specs):
        for sends, receives, copy in specs:
            @pl.when(receives)
            def _(copy=copy):
                copy.wait_recv()

            @pl.when(sends)
            def _(copy=copy):
                copy.wait_send()

    def colour_of(rnd, plane):
        cells = red_cells((half_y0, z0), plane)
        return jnp.logical_not(cells) if rnd == V0B else cells

    def start_wide(rnd, level, pad):
        ws, _, _, _, r, count, rows = buffers(rnd, level)
        if rnd != K0:
            for side, i in ((0, 0), (1, count - 1)):
                face = pad[i + 1, 8 : 8 + rows, :]
                if level == 0:
                    cells = colour_of(rnd, i)
                    face = jnp.where(cells, face[:half_y0], shift(face[half_y0:], 1, 1))
                ws[r, side] = face
        start_all(wide_copies(rnd, level))

    def start_narrow(rnd, level, pad):
        _, _, ns, _, r, count, rows = buffers(rnd, level)
        for i in range(count):
            ns[r, 0, i : i + 1, :] = pad[i + 1, 8:9, :]
            ns[r, 1, i : i + 1, :] = pad[i + 1, 7 + rows : 8 + rows, :]
        start_all(narrow_copies(rnd, level))

    def finish_wide(rnd, level, pad):
        _, wr, _, _, r, count, rows = buffers(rnd, level)
        finish_all(wide_copies(rnd, level))
        if rnd == K0:
            return
        for side, i in ((0, -1), (1, count)):
            @pl.when(w > 0 if side == 0 else w < wn - 1)
            def _(side=side, i=i):
                got = wr[r, side]
                if level == 0:
                    cells = colour_of(rnd, i)
                    upper, lower = pl.ds(8, half_y0), pl.ds(8 + half_y0, half_y0)
                    pad[i + 1, upper, :] = jnp.where(cells, got, pad[i + 1, upper, :])
                    pad[i + 1, lower, :] = jnp.where(
                        cells, shift(got, -1, 1), pad[i + 1, lower, :]
                    )
                else:
                    pad[i + 1, 8 : 8 + rows, :] = got

    def finish_narrow(rnd, level, pad):
        _, _, _, nr, r, count, rows = buffers(rnd, level)
        finish_all(narrow_copies(rnd, level))

        @pl.when(n > 0)
        def _():
            for i in range(count):
                pad[i + 1, 7:8, :] = nr[r, 0, i : i + 1, :]

        @pl.when(n < nn - 1)
        def _():
            for i in range(count):
                pad[i + 1, 8 + rows : 9 + rows, :] = nr[r, 1, i : i + 1, :]

    def halo_start(rnd, level, pad):
        start_wide(rnd, level, pad)
        start_narrow(rnd, level, pad)

    def halo_finish(rnd, level, pad):
        finish_narrow(rnd, level, pad)
        finish_wide(rnd, level, pad)

    pl.semaphore_wait(barrier, near)
    start_wide(K0, 0, kp0)
    meet_signal(0)
    k_in.wait()
    start_narrow(K0, 0, kp0)

    own1 = pl.ds(8, y1)

    def exists(a, c):
        good = None
        for side, at, size in ((a, w, wn), (c, n, nn)):
            if side is not None:
                here = at < size - 1 if side else at > 0
                good = here if good is None else jnp.logical_and(good, here)
        return good

    def copies1(rnd, array):
        specs = []

        def add(slot, a, c, src, dst, target):
            back = [None if side is None else 1 - side for side in (a, c)]
            specs.append((exists(a, c), exists(*back), pltpu.make_async_remote_copy(
                src_ref=src, dst_ref=dst, send_sem=hs1.at[rnd, slot],
                recv_sem=hr1.at[rnd, slot], device_id=target, device_id_type=MESH)))

        for a, c in corners:
            add(4 + 2 * a + c, a, c, cs1.at[rnd, a, c], cr1.at[rnd, 1 - a, 1 - c],
                diagonal(a, c))
        for side in (0, 1):
            if rnd == V1:
                src, dst = ws1.at[side], wr1.at[1 - side]
            else:
                src = array.at[pl.ds((2, x1)[side], 2), own1, :]
                dst = array.at[pl.ds((x1 + 2, 0)[side], 2), own1, :]
            add(side, side, None, src, dst, wide(1 if side else wn - 1))
        for side in (0, 1):
            add(2 + side, None, side, ns1.at[rnd, side], nr1.at[rnd, 1 - side],
                narrow(1 if side else nn - 1))
        return specs

    def start1(rnd, array):
        for a, c in corners:
            row = (8, 7 + y1)[c]
            cs1[rnd, a, c] = array[(2, x1 + 1)[a], row : row + 1, :]
        if rnd == V1:
            ws1[0] = array[2:4, 8 : 8 + y1, :]
            ws1[1] = array[x1 : x1 + 2, 8 : 8 + y1, :]
        for i in range(x1):
            ns1[rnd, 0, 2 * i : 2 * i + 2, :] = array[2 + i, 8:10, :]
            ns1[rnd, 1, 2 * i : 2 * i + 2, :] = array[2 + i, 6 + y1 : 8 + y1, :]
        start_all(copies1(rnd, array))

    def finish1(rnd, array):
        finish_all(copies1(rnd, array)[::-1])
        for side in (0, 1):
            if rnd == V1:
                @pl.when(exists(side, None))
                def _(side=side):
                    at = (0, x1 + 2)[side]
                    array[at : at + 2, 8 : 8 + y1, :] = wr1[side]

            @pl.when(exists(None, side))
            def _(side=side):
                at = (6, 8 + y1)[side]
                for i in range(x1):
                    array[2 + i, at : at + 2, :] = nr1[rnd, side, 2 * i : 2 * i + 2, :]

        for a, c in corners:
            @pl.when(exists(a, c))
            def _(a=a, c=c):
                at = (7, 8 + y1)[c]
                array[(1, x1 + 2)[a], at : at + 1, :] = cr1[rnd, a, c]

    def clear1(array):
        strip = jnp.zeros((8, z1), F32)
        for p in range(x1 + 4):
            array[p, 0:8, :] = strip
            array[p, 8 + y1 :, :] = strip

        for side in (0, 1):
            @pl.when(jnp.logical_not(exists(side, None)))
            def _(side=side):
                at = (0, x1 + 2)[side]
                array[at : at + 2, 8 : 8 + y1, :] = jnp.zeros((2, y1, z1), F32)

    def coefficients1():
        for j in range(1, x1 + 3):
            k = kp1[j]
            lane = iota(k.shape, 1)
            first, last = lane == 0, lane == z1 - 1
            faces = [kp1[j + 1], kp1[j - 1], shift(k, -1, 0), shift(k, 1, 0),
                     jnp.where(last, 0.0, shift(k, -1, 1)), jnp.where(first, 0.0, shift(k, 1, 1))]
            faces = [0.5 * (k + face) for face in faces]
            total = functools.reduce(lambda a, b: a + b, faces)
            inverse = jnp.where(k > 0.0, 1.0 / total, 0.0)
            for m, face in enumerate(faces):
                weight = face * inverse
                if m >= 4:
                    weight = jnp.where(first if m == 5 else last, 0.0, weight)
                w1[m, j] = weight
            d1[j] = total * 0.25
            f1[j] = 4.0 * inverse

    def updated1(j):
        v = v1[j]
        a = w1[0, j] * v1[j + 1] + w1[1, j] * v1[j - 1]
        b = w1[2, j] * shift(v, -1, 0) + w1[3, j] * shift(v, 1, 0)
        c = w1[4, j] * shift(v, -1, 1) + w1[5, j] * shift(v, 1, 1)
        return v, (s1[j] + a) + (b + c)

    def half_sweep1(planes, red):
        for j in planes:
            v, new = updated1(j)
            cells = red_cells(v.shape, j)
            v1[j] = jnp.where(cells, new, v) if red else jnp.where(cells, v, new)

    def gather_wide(g, which, local):
        copies = []
        for d in range(1, wn):
            copies.append(pltpu.make_async_remote_copy(
                src_ref=local, dst_ref=g.at[w, n],
                send_sem=gsa.at[which, d - 1], recv_sem=gra.at[which, d - 1],
                device_id=wide(d), device_id_type=MESH))
        return copies

    near_first = sorted(range(1, wn), key=lambda d: min(d, wn - d))

    def relay_copies(g, which, d, local):
        at = lax.rem(w + wn - d, wn)
        return [
            pltpu.make_async_remote_copy(
                src_ref=local if d == 0 else g.at[at, n], dst_ref=g.at[at, n],
                send_sem=gsb.at[which, d, e - 1], recv_sem=grb.at[which, d, e - 1],
                device_id=narrow(e), device_id_type=MESH)
            for e in range(1, nn)
        ]

    def gather_start(g, which, local):
        for copy in gather_wide(g, which, local)[::-1]:
            copy.start()
        for copy in relay_copies(g, which, 0, local):
            copy.start()

    def gather_relay(g, which, local):
        arriving = gather_wide(g, which, local)
        for d in near_first:
            arriving[d - 1].wait_recv()
            for copy in relay_copies(g, which, d, local):
                copy.start()

    def gather_finish(g, which, local):
        for d in [0] + near_first:
            for copy in relay_copies(g, which, d, local):
                copy.wait_recv()
        for d in [0] + near_first:
            for copy in relay_copies(g, which, d, local):
                copy.wait_send()
        for copy in gather_wide(g, which, local):
            copy.wait_send()

    for i in range(x1):
        for c, part in enumerate(restrict_pair(kp0[2 * i + 1, inside, :], kp0[2 * i + 2, inside, :], tmp, i % 2)):
            half0[i, :, pl.ds(c * 128, 128)] = part

    def lanes_down(half, store, planes, rows, cols):
        flat = half[...].reshape(planes * rows, cols)
        for c in range(cols // 256):
            got = matmul(flat[:, c * 256 : (c + 1) * 256], rmat[...]) * 0.125
            store(c, got.reshape(planes, rows, 128))

    def store_k1(c, got):
        k1[:, :, pl.ds(c * 128, 128)] = got
        kp1[2 : 2 + x1, 8 : 8 + y1, pl.ds(c * 128, 128)] = got

    lanes_down(half0, store_k1, x1, y1, z0)
    clear1(kp1)
    clear1(s1)
    start1(K1, kp1)
    for i in range(x2):
        for c, part in enumerate(restrict_pair(k1[2 * i], k1[2 * i + 1], tmp, i % 2)):
            half1[i, :, pl.ds(c * 128, 128)] = part

    def store_k2(c, got):
        k2l[...] = got
        gk[w, n] = got

    lanes_down(half1, store_k2, x2, y2, z1)
    clear(kp0, y0, ends=False)
    for pad, rows in ((v0, y0), (kp2, gy), (v2, gy)):
        clear(pad, rows)

    meet_wait(0)
    if len(meet_steps) > 1:
        meet_signal(1)
    b_in.wait()
    finish_narrow(K0, 0, kp0)
    finish_wide(K0, 0, kp0)
    level0 = (y0, x0, 2)
    for part in ("edge", "inner"):
        coefficients(kp0, w0, d0, s0, b_ref, 1.0, *level0, part=part)
        first_red(v0, s0, *level0, part=part)
        if part == "edge":
            start_wide(V0A, 0, v0)
    start_narrow(V0A, 0, v0)
    finish1(K1, kp1)
    coefficients1()
    for p in range(1, len(meet_steps)):
        meet_wait(p)
        if p + 1 < len(meet_steps):
            meet_signal(p + 1)
    gather_start(gk, 0, k2l)
    halo_finish(V0A, 0, v0)
    half_sweep(v0, w0, s0, *level0, False, part="edge")
    start_wide(V0B, 0, v0)
    half_sweep(v0, w0, s0, *level0, False, part="inner")
    start_narrow(V0B, 0, v0)
    gather_relay(gk, 0, k2l)
    finish_narrow(V0B, 0, v0)

    def residual(vpad, weights, scaled, diag, i, rows):
        v, new = updated(vpad, weights, scaled, i, rows)
        return diag[i] * (new - v)

    def restrict0(i, slot):
        first = residual(v0, w0, s0, d0, 2 * i, y0)
        second = residual(v0, w0, s0, d0, 2 * i + 1, y0)
        for c, part in enumerate(restrict_pair(first, second, tmp, slot)):
            half0[i, :, pl.ds(c * 128, 128)] = part

    @pl.loop(1, x1 - 1)
    def _(i):
        restrict0(i, 0)

    finish_wide(V0B, 0, v0)
    restrict0(0, 0)
    restrict0(x1 - 1, 1)

    def store_b1(c, got):
        b1[:, :, pl.ds(c * 128, 128)] = got

    lanes_down(half0, store_b1, x1, y1, z0)

    for i in range(x1):
        s1[2 + i, own1, :] = f1[2 + i, own1, :] * b1[i]
    start1(S1, s1)
    gather_finish(gk, 0, k2l)
    for a in range(wn):
        for c in range(nn):
            kp2[1 + a * x2 : 1 + (a + 1) * x2, 8 + c * y2 : 8 + (c + 1) * y2, :] = gk[a, c]
    coefficients(kp2, w2, d2, f2, None, 16.0, gy, gx, 8)

    def pack_down(get, tag):
        @pl.loop(0, px)
        def _(i):
            for h in (0, 1):
                part = restrict_pair(*get(i + h * px), tmp, h)[0]
                half2[i, :, pl.ds(h * 128, 128)] = part

        return matmul(half2[...].reshape(px * y3, 256), rmat[...]).reshape(px, y3, 128) * 0.125

    def plane_of(i):
        return kp2[1 + 2 * i, 8 : 8 + gy, :], kp2[2 + 2 * i, 8 : 8 + gy, :]

    k3 = pack_down(plane_of, 0)
    shape3 = (px, y3, 128)
    p_at, r_at, l_at = iota(shape3, 0), iota(shape3, 1), iota(shape3, 2)
    z_at = l_at & 63
    outside = [
        (p_at == px - 1) & (l_at >= 64),
        (p_at == 0) & (l_at < 64),
        r_at == y3 - 1,
        r_at == 0,
        z_at == 63,
        z_at == 0,
    ]

    def neighbours(v):
        xp = jnp.concatenate([v[1:], shift(v[:1], 64, 2)], axis=0)
        xm = jnp.concatenate([shift(v[-1:], 64, 2), v[:-1]], axis=0)
        return [xp, xm, shift(v, -1, 1), shift(v, 1, 1), shift(v, -1, 2), shift(v, 1, 2)]

    faces3 = [
        0.5 * (k3 + jnp.where(out, 0.0, near)) for out, near in zip(outside, neighbours(k3))
    ]
    total3 = functools.reduce(lambda a, b: a + b, faces3)
    inverse3 = 1.0 / total3
    for m in range(6):
        w3[m] = jnp.where(outside[m], 0.0, faces3[m] * inverse3)
    s3[...] = 64.0 * inverse3

    finish1(S1, s1)
    for j in range(x1 + 4):
        v1[j] = jnp.where(red_cells((y1 + 16, z1), j), s1[j], 0.0)
    half_sweep1(range(1, x1 + 3), False)

    def residual1(i):
        v, new = updated1(2 + i)
        return (d1[2 + i] * (new - v))[8 : 8 + y1]

    for i in range(x2):
        first, second = residual1(2 * i), residual1(2 * i + 1)
        for c, part in enumerate(restrict_pair(first, second, tmp, i % 2)):
            half1[i, :, pl.ds(c * 128, 128)] = part

    def store_b2(c, got):
        b2l[...] = got
        gb[w, n] = got

    lanes_down(half1, store_b2, x2, y2, z1)
    gather_start(gb, 1, b2l)

    gather_relay(gb, 1, b2l)
    gather_finish(gb, 1, b2l)

    for a in range(wn):
        for c in range(nn):
            for i in range(x2):
                rows = pl.ds(c * y2, y2)
                s2[a * x2 + i, rows, :] = f2[a * x2 + i, rows, :] * gb[a, c, i]
    first_red(v2, s2, gy, gx, 8)
    half_sweep(v2, w2, s2, gy, gx, 8, False)

    def resid2(i):
        return (residual(v2, w2, s2, d2, 2 * i, gy), residual(v2, w2, s2, d2, 2 * i + 1, gy))

    b3 = pack_down(resid2, 1)
    scaled3 = s3[...] * b3
    s3[...] = scaled3
    first_at = p_at + jnp.where(l_at >= 64, px, 0)
    red3 = ((first_at + r_at + z_at) & 1) == 0

    def sweep3(e, red):
        near = neighbours(e)
        terms = [w3[m] * near[m] for m in range(6)]
        new = ((s3[...] + terms[0]) + (terms[1] + terms[2])) + ((terms[3] + terms[4]) + terms[5])
        return jnp.where(red3, new, e) if red else jnp.where(red3, e, new)

    e = jnp.where(red3, scaled3, 0.0)
    e = sweep3(e, False)

    def sweeps3(_, e):
        for _ in range(5):
            e = sweep3(sweep3(e, True), False)
        return e

    e = lax.fori_loop(0, (CSWEEPS - 1) // 5, sweeps3, e)
    for _ in range((CSWEEPS - 1) % 5):
        e = sweep3(sweep3(e, True), False)

    wide3 = matmul(e.reshape(px * y3, 128), pmat[...]).reshape(px, y3, 256)
    for h in (0, 1):
        part = wide3[:, :, h * 128 : (h + 1) * 128]
        for i in range(px):
            up2[h * px + i, pl.ds(0, y3, 2), :] = part[i]
            up2[h * px + i, pl.ds(1, y3, 2), :] = part[i]

    def planes_from(first, count, limit):
        return jnp.clip(first, 0, limit - count)

    begin = planes_from(w * x2 // 2 - 2, x2 // 2 + 4, gx // 2)
    for m in range(x2 // 2 + 4):
        i = begin + m
        add = up2[i]
        for j in (1, 2):
            v2[2 * i + j, 8 : 8 + gy, :] = v2[2 * i + j, 8 : 8 + gy, :] + add

    for depth, red in ((2, True), (1, False)):
        count = x2 + 2 * depth
        begin = planes_from(w * x2 - depth, count, gx)
        for m in range(count):
            i = begin + m
            v, new = updated(v2, w2, s2, i, gy)
            cells = red_cells(v.shape, i)
            v2[i + 1, 8 : 8 + gy, :] = jnp.where(cells, new, v) if red else jnp.where(cells, v, new)

    def prolong(coarse, vpad, up, count, rows, depth):
        planes, crows, cols = coarse.shape
        flat = coarse.reshape(planes * crows, cols)
        span = (rows + 16) // 2
        for c in range(cols // 128):
            got = matmul(flat[:, c * 128 : (c + 1) * 128], pmat[...])
            got = got.reshape(planes, crows, 256)
            for i in range(planes):
                for q in (0, 1):
                    part = got[i, 4 : 4 + span, q * 128 : (q + 1) * 128]
                    up[i, 2 * c + q, pl.ds(0, span, 2), :] = part
                    up[i, 2 * c + q, pl.ds(1, span, 2), :] = part

        for p in range(count + 2 * depth):
            for c in range(cols // 64):
                lanes = pl.ds(c * 128, 128)
                vpad[p, :, lanes] = vpad[p, :, lanes] + up[(p + depth % 2) // 2, c]

    rows2 = pl.ds(pl.multiple_of(n * y2, 8), y2 + 16)
    prolong(v2[pl.ds(w * x2, x2 + 2), rows2, :], v1, up1, x1, y1, 2)
    half_sweep1(range(2, x1 + 2), True)
    start1(V1, v1)
    finish1(V1, v1)
    half_sweep1(range(1, x1 + 3), False)

    prolong(v1[1 : x1 + 3], v0, up0, x0, y0, 1)
    half_sweep(v0, w0, s0, *level0, True, part="edge")
    start_wide(V0C, 0, v0)
    half_sweep(v0, w0, s0, *level0, True, part="inner")
    start_narrow(V0C, 0, v0)
    finish_narrow(V0C, 0, v0)
    half_sweep(v0, w0, s0, *level0, False, out=out_ref, part="inner")
    results = [
        pltpu.make_async_copy(out_ref.at[planes], out_hbm.at[planes], ls.at[2 + m])
        for m, planes in enumerate((pl.ds(1, x0 - 2), pl.ds(0, 1), pl.ds(x0 - 1, 1)))
    ]
    results[0].start()
    finish_wide(V0C, 0, v0)
    half_sweep(v0, w0, s0, *level0, False, out=out_ref, part="edge")
    results[1].start()
    results[2].start()
    for copy in results:
        copy.wait()


def solution(mesh):
    wn, nn = mesh.shape["wide"], mesh.shape["narrow"]
    placed = P("wide", "narrow", None)

    def on_device(sources, permeability):
        x0, y0, z0 = sources.shape
        x1, y1, z1 = x0 // 2, y0 // 2, z0 // 2
        x2, y2, z2 = x1 // 2, y1 // 2, z1 // 2
        gx, gy = x2 * wn, y2 * nn
        px, y3 = gx // 4, gy // 2
        pad0, pad1, pad2 = (x0 + 2, y0 + 16, z0), (x1 + 4, y1 + 16, z1), (gx + 2, gy + 16, z2)
        l0, l1, l2 = (x0, y0, z0), (x1, y1, z1), (gx, gy, z2)
        v = lambda *shape: pltpu.VMEM(shape, F32)
        scratch = [
            v(*pad0), v(*pad0), v(6, *l0), v(*l0), v(*l0),
            v(*pad1), v(*pad1), v(6, *pad1), v(*pad1), v(*pad1), v(*pad1), v(*l1), v(*l1),
            v(*pad2), v(*pad2), v(6, *l2), v(*l2), v(*l2), v(*l2), v(x2, y2, z2), v(x2, y2, z2),
            v(wn, nn, x2, y2, z2), v(wn, nn, x2, y2, z2),
            v(6, px, y3, 128), v(px, y3, 128),
            v(2, z0 // 128, max(y0, gy), 128), v(x1, y1, z0), v(x2, y2, z1), v(px, y3, 256),
            v(x1 + 2, z0 // 128, y0 + 16, 128), v(x2 + 2, z1 // 128, y1 + 16, 128), v(gx // 2, gy, z2),
            pltpu.VMEM((256, 128), jnp.bfloat16), pltpu.VMEM((128, 256), jnp.bfloat16),
            v(4, 2, y0 // 2, z0), v(4, 2, y0 // 2, z0), v(4, 2, 8, z0), v(4, 2, 8, z0),
            v(2, 2, y1, z1), v(2, 2, y1, z1), v(3, 2, 2 * x1, z1), v(3, 2, 2 * x1, z1),
            v(3, 2, 2, 1, z1), v(3, 2, 2, 1, z1),
            pltpu.SemaphoreType.DMA((4, 4)), pltpu.SemaphoreType.DMA((4, 4)),
            pltpu.SemaphoreType.DMA((3, 8)), pltpu.SemaphoreType.DMA((3, 8)),
            pltpu.SemaphoreType.DMA((2, wn - 1)), pltpu.SemaphoreType.DMA((2, wn - 1)),
            pltpu.SemaphoreType.DMA((2, wn, nn - 1)), pltpu.SemaphoreType.DMA((2, wn, nn - 1)),
            v(*l0), v(*l0), pltpu.SemaphoreType.DMA((5,)), pltpu.SemaphoreType.REGULAR((16,)),
        ]
        return pl.pallas_call(
            functools.partial(kernel, (wn, nn)),
            out_shape=jax.ShapeDtypeStruct(sources.shape, F32),
            in_specs=[pl.BlockSpec(memory_space=pltpu.HBM)] * 2,
            out_specs=pl.BlockSpec(memory_space=pltpu.HBM),
            scratch_shapes=scratch,
            compiler_params=pltpu.CompilerParams(
                collective_id=0, has_side_effects=True, vmem_limit_bytes=60 * 1024 * 1024
            ),
        )(sources, permeability)

    return jax.shard_map(
        on_device, mesh=mesh, in_specs=(placed, placed), out_specs=placed, check_vma=False
    )
```
